256 devices in a mesh: snap: 4 (over x_hi, core), param: 64 (over x_lo, z, y).
Axes of the slice: x: 4 (x_hi: 2, x_lo: 2; x = x_hi * 2 + x_lo), y: 4, z: 8, core: 2. Of those that a mesh axis runs over, the one named last changes fastest.
Arguments:
- snap_in: float32 [32, 64, 1344], P('snap', None, 'param'), may hold values from -6 to 6
- snap_qkv: float32 [32, 1344, 4032], P('snap', 'param'), may hold values from -16 to 16
- snap_proj: float32 [32, 1344, 1344], P('snap', 'param'), may hold values from -16 to 16
- snap_out: float32 [32, 1344, 64], P('snap', 'param'), may hold values from -48 to 48
- coeffs: float32 [32, 8], P('snap'), may hold values from -3 to 3
- latent: float32 [64, 64, 256], P('param'), may hold values from -6 to 6
- levels: int32 [64], P('param'), may hold values from 0 to 15
Outputs:
- denoised: float32 [8, 64, 64, 256], P('snap', 'param')
The draws below stay inside these ranges and needn't reach their ends.
All inputs are finite; a program needn't handle non-finite values.
Results may differ from the reference program's by a relative error of at most 0.012.
Values may be sent and summed in bfloat16 or wider, within the bound.
No kernel may reach another device: no remote copies, remote signals or barrier semaphores. Data moves between devices by JAX's collectives and lax.ppermute only.
A program may use at most 192 MiB of HBM per device.

```python
import jax
import jax.numpy as jnp
from jax import lax

C = 1344
HEAD_DIM = 64
PROF = 8
SNAP_DEV = 8
NLEV = 16
SNAPS = 32
BATCH = 64
N_SNAP = 4
N_PARAM = 64


def draw_snap_out(key, part):
    base = jnp.clip(jax.random.normal(jax.random.fold_in(key, 11), (SNAPS, C, 64), jnp.float32), -6.0, 6.0)
    shift = jax.random.randint(jax.random.fold_in(key, 23), (), 0, N_PARAM)
    block = jnp.arange(C, dtype=jnp.int32) // (C // N_PARAM)
    column = jnp.arange(64, dtype=jnp.int32)
    paired = column[None, :] % N_PARAM == (block[:, None] + shift) % N_PARAM
    boost = jnp.where(paired, 8.0, 1.0).astype(jnp.float32)
    return base * boost[None, :, :]


def plant(drawn, key, least, top_value):
    place = [jax.random.randint(jax.random.fold_in(key, axis), (), 0, length) for axis, length in enumerate(drawn.shape)]
    longest = drawn.shape.index(max(drawn.shape))
    beside = place[:longest] + [(place[longest] + 1) % drawn.shape[longest]] + place[longest + 1:]
    return drawn.at[tuple(place)].set(least).at[tuple(beside)].set(top_value)


def raised(drawn, key, source, target, blocks, factor):
    def block_of(dim):
        return (jnp.arange(drawn.shape[dim]) // (drawn.shape[dim] // blocks)).reshape((-1,) + (1,) * (drawn.ndim - 1 - dim))

    first = jax.random.permutation(key, blocks)[block_of(target)]
    second = (block_of(target) + blocks // 2) % blocks
    return jnp.where((block_of(source) == first) | (block_of(source) == second), factor * drawn, drawn)


def shard_levels(rng, shape, pieces, least, top_value):
    loudness = 1.0
    for axis_at, blocks in pieces:
        heights = jax.random.uniform(jax.random.fold_in(jax.random.fold_in(rng, 6), axis_at), (blocks,), jnp.float32, least / len(pieces), top_value / len(pieces))
        loudness = loudness * jnp.repeat(jnp.exp(heights), shape[axis_at] // blocks).reshape((-1,) + (1,) * (len(shape) - 1 - axis_at))
    return loudness


def centred(key, extent, width, most, cuts=(), kind=jnp.bfloat16):
    entries = jax.random.normal(key, extent, jnp.float32) * width
    if len(cuts) > 0:
        entries = shard_levels(key, extent, cuts, -0.22, 0.18) * entries
    return jnp.clip(entries, min=-most, max=most).astype(kind)


def bell_draw_with(rng, dims, width, bound, split, heavy, kind=jnp.bfloat16):
    result = width * jax.random.normal(rng, dims, jnp.float32)
    if split:
        result = result * shard_levels(rng, dims, split, -0.22, 0.18)
    return jnp.clip(raised(result, jax.random.fold_in(rng, 3), *heavy), -bound, bound).astype(kind)


def setup_inputs(seed: int = 0) -> dict:
    key_list = jax.random.split(jax.random.key(seed), 8)
    return {
        "snap_in": centred(key_list[0], (SNAPS, 64, C), 1.0, 6.0, ((0, 4), (2, 64)), jnp.float32),
        "snap_qkv": bell_draw_with(key_list[1], (SNAPS, C, 3 * C), 1.0, 16.0, ((0, 4), (1, 64)), (1, 2, 64, 4.0), jnp.float32),
        "snap_proj": bell_draw_with(key_list[2], (SNAPS, C, C), 1.0, 16.0, ((0, 4), (1, 64)), (1, 2, 64, 4.0), jnp.float32),
        "snap_out": draw_snap_out(jax.random.fold_in(key_list[7], 71), 0),
        "coeffs": centred(key_list[4], (SNAPS, PROF), 0.5, 3.0, ((0, 4),), jnp.float32),
        "latent": centred(key_list[5], (BATCH, 64, 256), 1.0, 6.0, ((0, 64),), jnp.float32),
        "levels": plant(jax.random.randint(key_list[6], (BATCH,), 0, NLEV), jax.random.fold_in(key_list[6], 1), 0, NLEV - 1).astype(jnp.int32),
    }


EPS = 0.0001

def noise_scales(levels):
    step = levels.astype(jnp.float32) / (NLEV - 1)
    sigma = jnp.exp(jnp.log(0.2) + step * (jnp.log(5.0) - jnp.log(0.2)))
    square = sigma * sigma + 0.25
    return (1.0 / jnp.sqrt(square), 0.25 / square, 0.5 * sigma / jnp.sqrt(square))

def to_tokens(image):
    count = image.shape[0]
    parts = image.reshape(count, 16, 4, 16, 4, 4).transpose(0, 1, 3, 2, 4, 5)
    return parts.reshape(count, 256, 64)

def from_tokens(feature):
    count = feature.shape[0]
    parts = feature.reshape(count, 16, 16, 4, 4, 4).transpose(0, 1, 3, 2, 4, 5)
    return parts.reshape(count, 64, 256)

def column_unit(weights):
    norms = jnp.sqrt(lax.optimization_barrier(jnp.sum(weights * weights, axis=-2, keepdims=True)))
    return (weights / (EPS + norms)).astype(jnp.bfloat16)

def head_unit(values):
    scale = jnp.sqrt(lax.optimization_barrier(jnp.mean(values * values, axis=-1, keepdims=True)))
    return (values / (EPS + scale)).astype(jnp.bfloat16)

def forward(tokens, w_in, w_qkv, w_proj, w_out):
    rows = tokens.shape[0]
    count = rows // 256
    heads = C // HEAD_DIM
    hidden = jnp.dot(tokens, w_in, preferred_element_type=jnp.float32).astype(jnp.bfloat16)
    qkv = jnp.dot(hidden, w_qkv, preferred_element_type=jnp.float32)
    qkv = head_unit(qkv.reshape(count, 256, 3, heads, HEAD_DIM))
    query = qkv[:, :, 0].astype(jnp.float32)
    keys = qkv[:, :, 1].astype(jnp.float32)
    values = qkv[:, :, 2].astype(jnp.float32)
    scores = jnp.einsum('bqhd,bkhd->bhqk', query, keys) * (1.0 / jnp.sqrt(float(HEAD_DIM)))
    expo = jnp.exp(scores)
    weights = (expo / lax.optimization_barrier(jnp.sum(expo, axis=-1, keepdims=True))).astype(jnp.bfloat16)
    attended = jnp.einsum('bhqk,bkhd->bqhd', weights.astype(jnp.float32), values)
    attended = attended.astype(jnp.bfloat16).reshape(rows, C)
    projected = jnp.dot(attended, w_proj, preferred_element_type=jnp.float32)
    mixed = ((0.7 * hidden.astype(jnp.float32) + 0.3 * projected) / jnp.sqrt(0.58)).astype(jnp.bfloat16)
    return jnp.dot(mixed, w_out, preferred_element_type=jnp.float32)

def reference(snap_in, snap_qkv, snap_proj, snap_out, coeffs, latent, levels):
    groups = coeffs.reshape(N_SNAP, SNAP_DEV, PROF)

    def contract(snaps):
        total = None
        for group in range(N_SNAP):
            block = snaps[group * SNAP_DEV:(group + 1) * SNAP_DEV]
            part = jnp.einsum('sp,sij->pij', groups[group], block, precision=lax.Precision.HIGHEST)
            part = lax.optimization_barrier(part.astype(jnp.bfloat16)).astype(jnp.float32)
            total = part if total is None else total + part
        return total
    w_in = column_unit(contract(snap_in))
    w_qkv = column_unit(contract(snap_qkv))
    w_proj = column_unit(contract(snap_proj))
    w_out = column_unit(contract(snap_out))
    c_in, c_skip, c_out = noise_scales(levels)
    count = latent.shape[0]
    tokens = to_tokens(c_in[:, None, None] * latent).reshape(count * 256, 64).astype(jnp.bfloat16)

    def one_profile(weights):
        feature = forward(tokens, weights[0], weights[1], weights[2], weights[3])
        image = from_tokens(feature.reshape(count, 256, 64))
        return c_skip[:, None, None] * latent + c_out[:, None, None] * image
    return lax.map(one_profile, (w_in, w_qkv, w_proj, w_out))
```

```python
import jax
import jax.numpy as jnp
from jax import lax
from jax.sharding import Mesh, PartitionSpec as P

HEAD_DIM = 64
PROF = 8
NLEV = 16
EPS = 0.0001

SNAP = ("xh", "core")
PARAM = ("xl", "z", "y")
ZY = ("z", "y")
X = ("xh", "xl")


def noise_scales(levels):
    step = levels.astype(jnp.float32) / (NLEV - 1)
    sigma = jnp.exp(jnp.log(0.2) + step * (jnp.log(5.0) - jnp.log(0.2)))
    square = sigma * sigma + 0.25
    return (1.0 / jnp.sqrt(square), 0.25 / square, 0.5 * sigma / jnp.sqrt(square))


def to_tokens(image):
    return image.reshape(16, 4, 16, 4, 4).transpose(0, 2, 1, 3, 4).reshape(256, 64)


def from_tokens(feature):
    count = feature.shape[0]
    parts = feature.reshape(count, 16, 16, 4, 4, 4).transpose(0, 1, 3, 2, 4, 5)
    return parts.reshape(count, 64, 256)


def a2a(x, axis):
    return lax.all_to_all(x, axis, 0, 0, tiled=True)


def natural(rows):
    rows = rows.reshape(32, 2, 24, 64)[:, :, :21]
    return rows.transpose(1, 0, 2, 3).reshape(1344, 64)


def shards(snap_in, snap_qkv, snap_proj, snap_out, coeffs, latent, levels):
    f32, bf16 = jnp.float32, jnp.bfloat16
    mix = coeffs.reshape(8, 2, 2, 2).transpose(2, 1, 3, 0).reshape(8, 8)
    eye = jnp.eye(24, 21, dtype=f32)
    mix = (mix[:, None, None, :] * eye[None, :, :, None]).reshape(192, 168)

    def contract(x):
        return jnp.dot(mix, x, precision=lax.Precision.HIGHEST).astype(bf16)

    w_q = contract(snap_qkv.transpose(1, 0, 2).reshape(168, 4032))
    w_p = contract(snap_proj.transpose(1, 0, 2).reshape(168, 1344))
    w_o = contract(snap_out.transpose(1, 0, 2).reshape(168, 64))
    w_i = contract(snap_in.transpose(2, 0, 1).reshape(168, 64))
    pad = jnp.zeros((192, 64), bf16)
    part = jnp.concatenate([w_q, pad, w_p, pad, w_i, w_o], axis=1)

    part = a2a(part.reshape(2, 96, 5632), "core").astype(f32)
    part = (part[0] + part[1]).astype(bf16)
    part = a2a(part.reshape(4, 24, 5632), X).astype(f32)
    part = part.reshape(2, 48, 5632)
    total = part[0] + part[1]
    q, p, wi, wo = total[:, :4096], total[:, 4096:5440], total[:, 5504:5568], total[:, 5568:]
    wi = wi / (EPS + jnp.sqrt(jnp.sum(wi * wi, axis=1, keepdims=True)))
    ww = jnp.concatenate([wi, wo], axis=1).astype(bf16)
    squares = jnp.pad(jnp.sum(p * p, axis=0), (0, 64)).reshape(11, 128)
    squares = jnp.pad(squares, ((0, 5), (0, 0))).astype(bf16)
    q = q.astype(bf16).reshape(48, 32, 128).transpose(1, 0, 2)
    same = jnp.concatenate([ww, squares], axis=0)
    send = jnp.concatenate([q, jnp.broadcast_to(same[None], (32, 64, 128))], axis=1)
    got = a2a(send, ZY)

    q = got[:, :48].reshape(1536, 128)
    wi = got[:, 48:96, :64].reshape(1536, 64)
    wo = natural(got[:, 48:96, 64:])
    qf = q.astype(f32)
    qn = 1.0 / (EPS + jnp.sqrt(jnp.sum(qf * qf, axis=0)))
    m = lax.dot_general(wi, q, (((0,), (0,)), ((), ())), preferred_element_type=f32) * qn
    of = wo.astype(f32)
    on = 1.0 / (EPS + jnp.sqrt(jnp.sum(of * of, axis=0)))
    squares = jnp.sum(got[:, 96:107].astype(f32), axis=0).reshape(1408)[:1344]
    p = (p / (EPS + jnp.sqrt(squares))).astype(bf16)
    r = jnp.dot(p, wo, preferred_element_type=f32) * on
    n = lax.dot_general(natural(got[:, 48:96, :64]), wo, (((0,), (0,)), ((), ())), preferred_element_type=f32) * on
    r = r.reshape(2, 24, 64).transpose(1, 0, 2).reshape(24, 128)
    send = jnp.concatenate([m, r], axis=0).astype(bf16)
    got = a2a(jnp.broadcast_to(send[None], (32, 88, 128)), ZY)
    m = got[:, :64].transpose(1, 0, 2).reshape(64, 4096)[:, :4032]
    r = natural(got[:, 64:].reshape(32, 24, 2, 64).transpose(0, 2, 1, 3))

    c_in, c_skip, c_out = noise_scales(levels)
    tokens = to_tokens(c_in[:, None, None] * latent).astype(bf16)
    tokens = lax.all_gather(tokens, "xl", axis=0, tiled=True)
    qkv = jnp.dot(tokens, m, preferred_element_type=f32).reshape(2, 256, 3, 21, 64)
    scale = jnp.sqrt(jnp.mean(qkv * qkv, axis=-1, keepdims=True))
    qkv = (qkv / (EPS + scale)).astype(bf16)
    query, keys, values = qkv[:, :, 0], qkv[:, :, 1], qkv[:, :, 2]
    scores = jnp.einsum("bqhd,bkhd->bhqk", query, keys, preferred_element_type=f32)
    expo = jnp.exp(scores * (1.0 / jnp.sqrt(float(HEAD_DIM))))
    weights = (expo / jnp.sum(expo, axis=-1, keepdims=True)).astype(bf16)
    attended = jnp.einsum("bhqk,bkhd->bqhd", weights, values, preferred_element_type=f32)
    attended = attended.astype(bf16).reshape(512, 1344)
    feature = 0.3 * jnp.dot(attended, r, preferred_element_type=f32)
    feature = feature + 0.7 * jnp.dot(tokens, n.astype(bf16), preferred_element_type=f32)
    feature = feature * (1.0 / jnp.sqrt(0.58))

    feature = a2a(feature.reshape(2, 256, 64), "xl")
    image = from_tokens(feature)
    out = c_skip[:, None, None] * latent + c_out[:, None, None] * image
    return out[:, None]


def solution(mesh):
    fine = Mesh(mesh.devices.reshape(2, 2, 2, 8, 4), ("xh", "core", "xl", "z", "y"))
    in_specs = (
        P(SNAP, None, PARAM),
        P(SNAP, PARAM, None),
        P(SNAP, PARAM, None),
        P(SNAP, PARAM, None),
        P(SNAP, None),
        P(PARAM, None, None),
        P(PARAM),
    )
    out_specs = P(SNAP, PARAM, None, None)
    return jax.shard_map(shards, mesh=fine, in_specs=in_specs, out_specs=out_specs, check_vma=False)
```

```python
import jax
import jax.numpy as jnp
from jax import lax
from jax.experimental import pallas as pl
from jax.experimental.pallas import tpu as pltpu
from jax.sharding import Mesh, PartitionSpec as P

HEAD_DIM = 64
PROF = 8
NLEV = 16
EPS = 0.0001
LOG2E = 1.4426950408889634

SNAP = ("xh", "core")
PARAM = ("xl", "z", "y")
ZY = ("z", "y")
X = ("xh", "xl")
F32 = jnp.float32
BF16 = jnp.bfloat16
TN = (((0,), (0,)), ((), ()))


def noise_scales(levels):
    step = levels.astype(jnp.float32) / (NLEV - 1)
    sigma = jnp.exp(jnp.log(0.2) + step * (jnp.log(5.0) - jnp.log(0.2)))
    square = sigma * sigma + 0.25
    return (1.0 / jnp.sqrt(square), 0.25 / square, 0.5 * sigma / jnp.sqrt(square))


def a2a(x, axis):
    return lax.all_to_all(x, axis, 0, 0, tiled=True)


def contract_kernel(c_ref, q_ref, p_ref, i_ref, o_ref, out_ref):
    snap = lax.broadcasted_iota(jnp.int32, (8, 168), 0)
    col = lax.broadcasted_iota(jnp.int32, (8, 168), 1)
    pick = jnp.where(lax.rem(col, 8) == snap, 1.0, 0.0)
    rows = lax.dot_general(c_ref[...], pick, TN, precision=lax.Precision.HIGHEST,
                           preferred_element_type=F32)
    r = lax.broadcasted_iota(jnp.int32, (24, 168), 0)
    col = lax.broadcasted_iota(jnp.int32, (24, 168), 1)
    same = jnp.where(col // 8 == r, 1.0, 0.0)
    mix = jnp.concatenate([rows[p:p + 1] * same for p in range(8)], axis=0)
    mix_hi = mix.astype(BF16)
    mix_lo = (mix - mix_hi.astype(F32)).astype(BF16)

    def piece(ref, start, width, at):
        x = ref[:, start:start + width]
        hi = x.astype(BF16)
        lo = (x - hi.astype(F32)).astype(BF16)
        y = jnp.dot(mix_hi, hi, preferred_element_type=F32)
        y = y + jnp.dot(mix_hi, lo, preferred_element_type=F32)
        y = y + jnp.dot(mix_lo, hi, preferred_element_type=F32)
        y = y.astype(BF16)
        for p in range(8):
            core, slot = (p // 2) % 2, (p // 4) * 2 + p % 2
            out_ref[core, slot * 24:slot * 24 + 24, at:at + width] = y[p * 24:p * 24 + 24]

    for k in range(7):
        piece(q_ref, 512 * k, 512, 512 * k)
    piece(q_ref, 3584, 448, 3584)
    for k in range(2):
        piece(p_ref, 512 * k, 512, 4096 + 512 * k)
    piece(p_ref, 1024, 320, 5120)
    piece(i_ref, 0, 64, 5504)
    piece(o_ref, 0, 64, 5568)
    out_ref[:, :, 4032:4096] = jnp.zeros((2, 96, 64), BF16)
    out_ref[:, :, 5440:5504] = jnp.zeros((2, 96, 64), BF16)


def contract(coeffs, q, p, w_in, w_out):
    return pl.pallas_call(
        contract_kernel,
        out_shape=jax.ShapeDtypeStruct((2, 96, 5632), BF16),
        name="contract",
        cost_estimate=pl.CostEstimate(flops=3 * 2 * 192 * 168 * 5504, bytes_accessed=6000000,
                                      transcendentals=0),
    )(coeffs, q, p, w_in, w_out)


def attend_kernel(t_ref, b_ref, r_ref, n_ref, o_ref, s_ref, a_ref, z_ref):
    tokens = jnp.concatenate([t_ref[0], t_ref[1]], axis=1)

    def project(c, carry):
        x = lax.dot_general(b_ref[c, 0:64, :], tokens, TN, preferred_element_type=F32)
        x = x.reshape(2, 64, 512)
        scale = jnp.sqrt(jnp.sum(x * x, axis=1, keepdims=True) * (1.0 / 64))
        s_ref[pl.ds(2 * c, 2)] = (x * (1.0 / (EPS + scale))).astype(BF16)
        return carry

    lax.fori_loop(0, 32, project, 0, unroll=4)

    def head(h, carry):
        for b in range(2):
            at = slice(256 * b, 256 * b + 256)
            query, keys, values = s_ref[h, :, at], s_ref[21 + h, :, at], s_ref[42 + h, :, at]
            scores = lax.dot_general(keys, query, TN, preferred_element_type=F32)
            expo = jnp.exp2(scores * (0.125 * LOG2E))
            total = jnp.sum(expo, axis=0, keepdims=True)
            out = jnp.dot(values, expo.astype(BF16), preferred_element_type=F32)
            a_ref[pl.ds(pl.multiple_of(h * 64, 64), 64), at] = (out * (1.0 / total)).astype(BF16)
        return carry

    lax.fori_loop(0, 21, head, 0, unroll=3)

    feature = 0.3 * lax.dot_general(r_ref[...], a_ref[...], TN, preferred_element_type=F32)
    feature = feature + 0.7 * lax.dot_general(n_ref[...], tokens, TN, preferred_element_type=F32)
    feature = feature * (1.0 / (0.58 ** 0.5))
    token = lax.broadcasted_iota(jnp.int32, (256, 256), 0)
    lane = lax.broadcasted_iota(jnp.int32, (256, 256), 1)
    keep = lax.rem(token, 16) == lane // 16
    row = lax.broadcasted_iota(jnp.int32, (128, 256), 0)
    lane = lax.broadcasted_iota(jnp.int32, (128, 256), 1)
    for b in range(2):
        part = feature[:, 256 * b:256 * b + 256]
        hi = part.astype(BF16)
        lo = (part - hi.astype(F32)).astype(BF16)
        both = jnp.concatenate([hi, lo], axis=0)
        for i in range(4):
            tile = jnp.where(lax.rem(row, 64) == 16 * i + lax.rem(lane, 16), 1.0, 0.0).astype(BF16)
            wide = lax.dot_general(both, tile, TN, preferred_element_type=F32)
            wide = jnp.where(keep, wide, 0.0).reshape(16, 16, 256)
            wide = jnp.sum(wide, axis=1)
            z_ref[2 * b, pl.ds(i, 16, stride=4), :] = wide[:, :128]
            z_ref[2 * b + 1, pl.ds(i, 16, stride=4), :] = wide[:, 128:]
        o_ref[b] = jnp.concatenate([z_ref[2 * b], z_ref[2 * b + 1]], axis=1)


def attend(tokens, got, r, n):
    return pl.pallas_call(
        attend_kernel,
        out_shape=jax.ShapeDtypeStruct((2, 64, 256), F32),
        scratch_shapes=[pltpu.VMEM((64, 64, 512), BF16), pltpu.VMEM((1344, 512), BF16),
                        pltpu.VMEM((4, 64, 128), F32)],
        name="attend",
        cost_estimate=pl.CostEstimate(flops=1000000000, bytes_accessed=1200000, transcendentals=2800000),
    )(tokens, got, r, n)


def natural(rows):
    return rows.reshape(32, 2, 21, 64).transpose(1, 0, 2, 3).reshape(1344, 64)


def shards(snap_in, snap_qkv, snap_proj, snap_out, coeffs, latent, levels):
    part = contract(
        coeffs,
        snap_qkv.transpose(1, 0, 2).reshape(168, 4032),
        snap_proj.transpose(1, 0, 2).reshape(168, 1344),
        snap_in.transpose(2, 0, 1).reshape(168, 64),
        snap_out.transpose(1, 0, 2).reshape(168, 64),
    )
    part = a2a(part, "core").astype(F32)
    part = (part[0] + part[1]).astype(BF16)
    part = a2a(part.reshape(4, 24, 5632), X).astype(F32)
    part = part.reshape(2, 2, 24, 5632)
    total = (part[0] + part[1])[:, :21].reshape(42, 5632)
    q, p, wi, wo = total[:, :4096], total[:, 4096:5440], total[:, 5504:5568], total[:, 5568:]
    wi = wi / (EPS + jnp.sqrt(jnp.sum(wi * wi, axis=1, keepdims=True)))
    ww = jnp.concatenate([wi, wo], axis=1)
    squares = jnp.pad(jnp.sum(p * p, axis=0), (0, 64)).reshape(11, 128)
    q = q.reshape(42, 32, 128).transpose(1, 0, 2)
    same = jnp.concatenate([ww, squares, jnp.zeros((1, 128), F32)], axis=0)
    send = jnp.concatenate([q, jnp.broadcast_to(same[None], (32, 54, 128))], axis=1).astype(BF16)
    got = a2a(send, ZY)

    q = got[:, :42].reshape(1344, 128)
    wi = got[:, 42:84, :64].reshape(1344, 64)
    wo = got[:, 42:84, 64:].reshape(1344, 64)
    qf = q.astype(F32)
    qn = 1.0 / (EPS + jnp.sqrt(jnp.sum(qf * qf, axis=0)))
    m = lax.dot_general(wi, q, TN, preferred_element_type=F32) * qn
    of = wo.astype(F32)
    on = 1.0 / (EPS + jnp.sqrt(jnp.sum(of * of, axis=0)))
    squares = jnp.sum(got[:, 84:95].astype(F32), axis=0).reshape(1408)[:1344]
    p = (p / (EPS + jnp.sqrt(squares))).astype(BF16)
    r = jnp.dot(p, natural(wo), preferred_element_type=F32) * on
    n = lax.dot_general(wi, wo, TN, preferred_element_type=F32) * on
    r = jnp.pad(r.reshape(2, 21, 64), ((0, 0), (0, 3), (0, 0)))
    r = jnp.concatenate([r[0], r[1]], axis=1)
    send = jnp.concatenate([m, r], axis=0).astype(BF16)
    got = a2a(jnp.broadcast_to(send[None], (32, 88, 128)), ZY)
    r = got[:, 64:85]
    r = jnp.concatenate([r[:, :, :64], r[:, :, 64:]], axis=0).reshape(1344, 64)

    c_in, c_skip, c_out = noise_scales(levels)
    tokens = (c_in[:, None, None] * latent).astype(BF16)
    tokens = tokens.reshape(16, 4, 16, 16).transpose(1, 3, 0, 2).reshape(1, 64, 256)
    tokens = lax.all_gather(tokens, "xl", axis=0, tiled=True)
    feature = a2a(attend(tokens, got, r, n.astype(BF16)), "xl")
    out = c_skip[:, None, None] * latent + c_out[:, None, None] * feature
    return out[:, None]


def solution(mesh):
    fine = Mesh(mesh.devices.reshape(2, 2, 2, 8, 4), ("xh", "core", "xl", "z", "y"))
    in_specs = (
        P(SNAP, None, PARAM),
        P(SNAP, PARAM, None),
        P(SNAP, PARAM, None),
        P(SNAP, PARAM, None),
        P(SNAP, None),
        P(PARAM, None, None),
        P(PARAM),
    )
    out_specs = P(SNAP, PARAM, None, None)
    return jax.shard_map(shards, mesh=fine, in_specs=in_specs, out_specs=out_specs, check_vma=False)
```

```python
import jax
import jax.numpy as jnp
from jax import lax
from jax.experimental import pallas as pl
from jax.experimental.pallas import tpu as pltpu
from jax.sharding import Mesh, PartitionSpec as P

HEAD_DIM = 64
PROF = 8
NLEV = 16
EPS = 0.0001
LOG2E = 1.4426950408889634

SNAP = ("xh", "core")
PARAM = ("xl", "z", "y")
ZY = ("z", "y")
X = ("xh", "xl")
F32 = jnp.float32
BF16 = jnp.bfloat16
TN = (((0,), (0,)), ((), ()))


def noise_scales(levels):
    step = levels.astype(jnp.float32) / (NLEV - 1)
    sigma = jnp.exp(jnp.log(0.2) + step * (jnp.log(5.0) - jnp.log(0.2)))
    square = sigma * sigma + 0.25
    return (1.0 / jnp.sqrt(square), 0.25 / square, 0.5 * sigma / jnp.sqrt(square))


def a2a(x, axis):
    return lax.all_to_all(x, axis, 0, 0, tiled=True)


def contract_kernel(c_ref, q_ref, p_ref, i_ref, o_ref, m_ref, h_ref):
    snap = lax.broadcasted_iota(jnp.int32, (8, 168), 0)
    col = lax.broadcasted_iota(jnp.int32, (8, 168), 1)
    pick = jnp.where(lax.rem(col, 8) == snap, 1.0, 0.0)
    rows = lax.dot_general(c_ref[...], pick, TN, precision=lax.Precision.HIGHEST,
                           preferred_element_type=F32)
    r = lax.broadcasted_iota(jnp.int32, (24, 168), 0)
    col = lax.broadcasted_iota(jnp.int32, (24, 168), 1)
    same = jnp.where(col // 8 == r, 1.0, 0.0)
    mix = jnp.concatenate([rows[p:p + 1] * same for p in range(8)], axis=0)
    mix_hi = mix.astype(BF16)
    mix_lo = (mix - mix_hi.astype(F32)).astype(BF16)

    def piece(x):
        hi = x.astype(BF16)
        lo = (x - hi.astype(F32)).astype(BF16)
        y = jnp.dot(mix_hi, hi, preferred_element_type=F32)
        y = y + jnp.dot(mix_hi, lo, preferred_element_type=F32)
        y = y + jnp.dot(mix_lo, hi, preferred_element_type=F32)
        return y.astype(BF16)

    def store(y, blocks, at):
        width = y.shape[1]
        for p in range(8):
            core, slot = (p // 2) % 2, (p // 4) * 2 + p % 2
            for block in blocks:
                m_ref[core, 4 * slot + block, :, at:at + width] = y[p * 24:p * 24 + 24]

    store(piece(jnp.concatenate([i_ref[...], o_ref[...]], axis=1)), range(4), 1408)
    for start, width in ((0, 512), (512, 512), (1024, 320)):
        h_ref[:, start:start + width] = piece(p_ref[:, start:start + width])
    source = lax.broadcasted_iota(jnp.int32, (1344, 384), 0)
    col = lax.broadcasted_iota(jnp.int32, (1, 384), 1)
    r = lax.rem(col, 24)
    for block in range(4):
        want = jnp.where(r < 21, (col // 24) * 84 + block * 21 + r, -1)
        order = jnp.where(source == want, 1.0, 0.0).astype(BF16)
        y = jnp.dot(h_ref[...], order, preferred_element_type=F32).astype(BF16)
        store(y, (block,), 1024)
    for k in range(8):
        width = 512 if k < 7 else 448
        store(piece(q_ref[:, 512 * k:512 * k + width]), (k // 2,), 512 * (k % 2))
    for slot in range(4):
        m_ref[:, 4 * slot + 3, :, 960:1024] = jnp.zeros((2, 24, 64), BF16)


def contract(coeffs, q, p, w_in, w_out):
    return pl.pallas_call(
        contract_kernel,
        out_shape=jax.ShapeDtypeStruct((2, 16, 24, 1536), BF16),
        scratch_shapes=[pltpu.VMEM((192, 1344), BF16)],
        name="contract",
        compiler_params=pltpu.CompilerParams(vmem_limit_bytes=16 << 20),
        cost_estimate=pl.CostEstimate(flops=3 * 2 * 192 * 168 * 5504, bytes_accessed=6000000,
                                      transcendentals=0),
    )(coeffs, q, p, w_in, w_out)


def lines(values, count, width):
    hi = values.astype(BF16).astype(F32)
    lo = values - hi
    parts = [x[:, width * k:width * k + width] for x in (hi, lo) for k in range(count)]
    row = lax.broadcasted_iota(jnp.int32, (8, width), 0)
    out = jnp.zeros((8, width), F32)
    for k, part in enumerate(parts):
        out = jnp.where(row == k, part, out)
    return out


def unlines(rows, count):
    return jnp.concatenate([rows[k:k + 1] + rows[count + k:count + k + 1] for k in range(count)],
                           axis=1)


def partial_kernel(y_ref, g_ref, o_ref, p_ref):
    total = (g_ref[0:8].astype(F32) + g_ref[8:16].astype(F32)).reshape(192, 1536)
    w_in = total[:, 1408:1472]
    norm = jnp.sqrt(jnp.sum(w_in * w_in, axis=1, keepdims=True))
    w_in = (w_in / (EPS + norm)).astype(BF16)
    w_out = total[:, 1472:1536].astype(BF16)
    n = lax.dot_general(w_in, w_out, TN, preferred_element_type=F32)
    proj = total[:, 1024:1408]
    p_ref[...] = proj
    y = y_ref[0]
    own = [g_ref[4 * x + y].astype(F32) + g_ref[8 + 4 * x + y].astype(F32) for x in range(2)]
    own = jnp.concatenate([x[:, 1472:1536] for x in own], axis=1)
    low = jnp.concatenate([own, lines(jnp.sum(proj * proj, axis=0, keepdims=True), 3, 128)], axis=0)
    for z in range(8):
        q = total[:, 128 * z:128 * z + 128]
        m = lax.dot_general(w_in, q.astype(BF16), TN, preferred_element_type=F32)
        side = lines(jnp.sum(q * q, axis=0, keepdims=True), 2, 64)
        tail = jnp.concatenate([n[8 * z:8 * z + 8], side], axis=1)
        o_ref[z] = jnp.concatenate([m, tail, low], axis=0).astype(BF16)


def partial_products(y, got):
    return pl.pallas_call(
        partial_kernel,
        out_shape=(jax.ShapeDtypeStruct((8, 104, 128), BF16),
                   jax.ShapeDtypeStruct((192, 384), F32)),
        in_specs=[pl.BlockSpec(memory_space=pltpu.SMEM), pl.BlockSpec(memory_space=pltpu.VMEM)],
        name="partial",
        compiler_params=pltpu.CompilerParams(vmem_limit_bytes=8 << 20),
        cost_estimate=pl.CostEstimate(flops=2 * 64 * 192 * 1152, bytes_accessed=1000000,
                                      transcendentals=0),
    )(y, got)


def whole_kernel(g_ref, p_ref, o_ref, r_ref):
    total = g_ref[0].astype(F32)
    for z in range(1, 8):
        total = total + g_ref[z].astype(F32)
    m = total[0:64] / (EPS + jnp.sqrt(unlines(total[64:72, 64:128], 2)))
    out = jnp.concatenate([m, total[64:72]], axis=0).astype(BF16)
    for k in range(32):
        o_ref[k] = out
    w_out = g_ref[:, 72:96, :].astype(F32).reshape(192, 128)
    w_out = jnp.concatenate([w_out[:, :64], w_out[:, 64:]], axis=0)
    norm = jnp.sqrt(unlines(total[96:104], 3))
    proj = (p_ref[...] / (EPS + norm)).astype(BF16)
    r = jnp.dot(proj, w_out.astype(BF16), preferred_element_type=F32)
    square = lines(jnp.sum(w_out * w_out, axis=0, keepdims=True), 1, 64)
    square = jnp.concatenate([square, square], axis=1)
    for y in range(4):
        both = jnp.concatenate([r[24 * y:24 * y + 24], r[96 + 24 * y:120 + 24 * y]], axis=1)
        r_ref[y] = jnp.concatenate([both, square], axis=0).astype(BF16)


def whole_products(got, proj):
    return pl.pallas_call(
        whole_kernel,
        out_shape=(jax.ShapeDtypeStruct((32, 72, 128), BF16),
                   jax.ShapeDtypeStruct((4, 32, 128), BF16)),
        name="whole",
        compiler_params=pltpu.CompilerParams(vmem_limit_bytes=8 << 20),
        cost_estimate=pl.CostEstimate(flops=100000, bytes_accessed=800000, transcendentals=0),
    )(got, proj)


def attend_kernel(t_ref, b_ref, a_ref, s_ref):
    tokens = jnp.concatenate([t_ref[0], t_ref[1]], axis=1)

    def project(c, carry):
        x = lax.dot_general(b_ref[c, 0:64, :], tokens, TN, preferred_element_type=F32)
        x = x.reshape(2, 64, 512)
        scale = jnp.sqrt(jnp.sum(x * x, axis=1, keepdims=True) * (1.0 / 64))
        unit = 2 * (lax.rem(c, 4) * 8 + c // 4)
        s_ref[pl.ds(unit, 2)] = (x * (1.0 / (EPS + scale))).astype(BF16)
        return carry

    lax.fori_loop(0, 32, project, 0, unroll=4)

    def head(h, carry):
        for b in range(2):
            at = slice(256 * b, 256 * b + 256)
            query, keys, values = s_ref[h, :, at], s_ref[21 + h, :, at], s_ref[42 + h, :, at]
            scores = lax.dot_general(keys, query, TN, preferred_element_type=F32)
            expo = jnp.exp2(scores * (0.125 * LOG2E))
            total = jnp.sum(expo, axis=0, keepdims=True)
            out = jnp.dot(values, expo.astype(BF16), preferred_element_type=F32)
            a_ref[pl.ds(pl.multiple_of(h * 64, 64), 64), at] = (out * (1.0 / total)).astype(BF16)
        return carry

    lax.fori_loop(0, 21, head, 0, unroll=3)


def attend(tokens, got):
    return pl.pallas_call(
        attend_kernel,
        out_shape=jax.ShapeDtypeStruct((1344, 512), BF16),
        scratch_shapes=[pltpu.VMEM((64, 64, 512), BF16)],
        name="attend",
        compiler_params=pltpu.CompilerParams(vmem_limit_bytes=16 << 20),
        cost_estimate=pl.CostEstimate(flops=5000000000, bytes_accessed=2400000, transcendentals=2800000),
    )(tokens, got)


def output_kernel(t_ref, b_ref, a_ref, r_ref, s_out_ref, o_ref, z_ref):
    tokens = jnp.concatenate([t_ref[0], t_ref[1]], axis=1)
    feature = 0.3 * lax.dot_general(r_ref[...], a_ref[...], TN, preferred_element_type=F32)
    n = jnp.concatenate([b_ref[4 * z, 64:72, 0:64].astype(F32) for z in range(8)], axis=0)
    feature = feature + 0.7 * lax.dot_general(n.astype(BF16), tokens, TN, preferred_element_type=F32)
    feature = feature * (s_out_ref[...] * (1.0 / (0.58 ** 0.5)))
    token = lax.broadcasted_iota(jnp.int32, (256, 256), 0)
    lane = lax.broadcasted_iota(jnp.int32, (256, 256), 1)
    keep = lax.rem(token, 16) == lane // 16
    row = lax.broadcasted_iota(jnp.int32, (128, 256), 0)
    lane = lax.broadcasted_iota(jnp.int32, (128, 256), 1)
    for b in range(2):
        part = feature[:, 256 * b:256 * b + 256]
        hi = part.astype(BF16)
        lo = (part - hi.astype(F32)).astype(BF16)
        both = jnp.concatenate([hi, lo], axis=0)
        for i in range(4):
            tile = jnp.where(lax.rem(row, 64) == 16 * i + lax.rem(lane, 16), 1.0, 0.0).astype(BF16)
            wide = lax.dot_general(both, tile, TN, preferred_element_type=F32)
            wide = jnp.where(keep, wide, 0.0).reshape(16, 16, 256)
            wide = jnp.sum(wide, axis=1)
            z_ref[2 * b, pl.ds(i, 16, stride=4), :] = wide[:, :128]
            z_ref[2 * b + 1, pl.ds(i, 16, stride=4), :] = wide[:, 128:]
        o_ref[b] = jnp.concatenate([z_ref[2 * b], z_ref[2 * b + 1]], axis=1)


def output(tokens, got, attended, r, scale):
    return pl.pallas_call(
        output_kernel,
        out_shape=jax.ShapeDtypeStruct((2, 64, 256), F32),
        scratch_shapes=[pltpu.VMEM((4, 64, 128), F32)],
        name="output",
        compiler_params=pltpu.CompilerParams(vmem_limit_bytes=12 << 20),
        cost_estimate=pl.CostEstimate(flops=100000000, bytes_accessed=2000000, transcendentals=0),
    )(tokens, got, attended, r, scale)


def shards(snap_in, snap_qkv, snap_proj, snap_out, coeffs, latent, levels):
    y = lax.axis_index("y")
    part = contract(
        coeffs,
        snap_qkv.transpose(1, 0, 2).reshape(168, 4032),
        snap_proj.transpose(1, 0, 2).reshape(168, 1344),
        snap_in.transpose(2, 0, 1).reshape(168, 64),
        snap_out.transpose(1, 0, 2).reshape(168, 64),
    )
    part = a2a(part, "core").astype(F32)
    part = (part[0] + part[1]).astype(BF16)
    part = a2a(part, ("xh", "xl", "y"))
    send, proj = partial_products(y.astype(jnp.int32).reshape(1), part)
    send, side = whole_products(a2a(send, "z"), proj)
    got = a2a(send, ZY)

    total = lax.dynamic_index_in_dim(side, y, 0, False).astype(F32)
    for d in range(1, 4):
        there = lax.dynamic_index_in_dim(side, lax.rem(y + d, 4), 0, False)
        there = lax.ppermute(there, "y", [(k, (k + d) % 4) for k in range(4)])
        total = total + there.astype(F32)
    scale = 1.0 / (EPS + jnp.sqrt(total[24, :64] + total[25, :64]))
    total, _ = lax.optimization_barrier((total, got))
    r = jnp.broadcast_to(total[None, :24].astype(BF16), (32, 24, 128))
    r = a2a(r, ZY)[:, :21]
    r = jnp.concatenate([r[:, :, :64], r[:, :, 64:]], axis=0).reshape(1344, 64)

    c_in, c_skip, c_out = noise_scales(levels)
    tokens = (c_in[:, None, None] * latent).astype(BF16)
    tokens = tokens.reshape(16, 4, 16, 16).transpose(1, 3, 0, 2).reshape(1, 64, 256)
    tokens = lax.all_gather(tokens, "xl", axis=0, tiled=True)
    attended = attend(tokens, got)
    feature = a2a(output(tokens, got, attended, r, scale[:, None]), "xl")
    out = c_skip[:, None, None] * latent + c_out[:, None, None] * feature
    return out[:, None]


def solution(mesh):
    fine = Mesh(mesh.devices.reshape(2, 2, 2, 8, 4), ("xh", "core", "xl", "z", "y"))
    in_specs = (
        P(SNAP, None, PARAM),
        P(SNAP, PARAM, None),
        P(SNAP, PARAM, None),
        P(SNAP, PARAM, None),
        P(SNAP, None),
        P(PARAM, None, None),
        P(PARAM),
    )
    out_specs = P(SNAP, PARAM, None, None)
    return jax.shard_map(shards, mesh=fine, in_specs=in_specs, out_specs=out_specs, check_vma=False)
```

```python
import jax
import jax.numpy as jnp
from jax import lax
from jax.experimental import pallas as pl
from jax.experimental.pallas import tpu as pltpu
from jax.sharding import Mesh, PartitionSpec as P

HEAD_DIM = 64
PROF = 8
NLEV = 16
EPS = 0.0001
LOG2E = 1.4426950408889634

SNAP = ("xh", "core")
PARAM = ("xl", "z", "y")
ZY = ("z", "y")
X = ("xh", "xl")
F32 = jnp.float32
BF16 = jnp.bfloat16
TN = (((0,), (0,)), ((), ()))


def noise_scales(levels):
    step = levels.astype(jnp.float32) / (NLEV - 1)
    sigma = jnp.exp(jnp.log(0.2) + step * (jnp.log(5.0) - jnp.log(0.2)))
    square = sigma * sigma + 0.25
    return (1.0 / jnp.sqrt(square), 0.25 / square, 0.5 * sigma / jnp.sqrt(square))


def a2a(x, axis):
    return lax.all_to_all(x, axis, 0, 0, tiled=True)


def contract_kernel(c_hbm, q_hbm, p_hbm, i_hbm, o_hbm, keep_ref, give_ref, q_ref, p_ref, i_ref,
                    o_ref, h_ref, c_ref, sems):
    copies = [pltpu.make_async_copy(a, b, sems.at[k]) for k, (a, b) in enumerate(
        ((i_hbm, i_ref), (o_hbm, o_ref), (p_hbm, p_ref), (q_hbm, q_ref), (c_hbm, c_ref)))]
    for k in (4, 0, 1, 2, 3):
        copies[k].start()
    copies[4].wait()
    snap = lax.broadcasted_iota(jnp.int32, (8, 168), 0)
    col = lax.broadcasted_iota(jnp.int32, (8, 168), 1)
    pick = jnp.where(lax.rem(col, 8) == snap, 1.0, 0.0)
    rows = lax.dot_general(c_ref[...], pick, TN, precision=lax.Precision.HIGHEST,
                           preferred_element_type=F32)
    r = lax.broadcasted_iota(jnp.int32, (24, 168), 0)
    col = lax.broadcasted_iota(jnp.int32, (24, 168), 1)
    same = jnp.where(col // 8 == r, 1.0, 0.0)
    mine = lax.axis_index("core")
    picked = []
    for k in range(2):
        for slot in range(4):
            p = (slot // 2) * 4 + slot % 2
            picked.append(jnp.where(mine == k, rows[p:p + 1], rows[p + 2:p + 3]))
    mix = jnp.concatenate([row * same for row in picked], axis=0)
    mix_hi = mix.astype(BF16)
    mix_lo = (mix - mix_hi.astype(F32)).astype(BF16)

    def piece(x):
        hi = x.astype(BF16)
        lo = (x - hi.astype(F32)).astype(BF16)
        y = jnp.dot(mix_hi, hi, preferred_element_type=F32)
        y = y + jnp.dot(mix_hi, lo, preferred_element_type=F32)
        y = y + jnp.dot(mix_lo, hi, preferred_element_type=F32)
        return y.astype(BF16)

    def store(y, blocks, at):
        width = y.shape[1]
        for k, ref in enumerate((keep_ref, give_ref)):
            for slot in range(4):
                row = 96 * k + 24 * slot
                for block in blocks:
                    ref[4 * slot + block, :, at:at + width] = y[row:row + 24]

    copies[0].wait()
    copies[1].wait()
    store(piece(jnp.concatenate([i_ref[...], o_ref[...]], axis=1)), range(4), 1408)
    copies[2].wait()
    for start, width in ((0, 512), (512, 512), (1024, 320)):
        h_ref[:, start:start + width] = piece(p_ref[:, start:start + width])
    source = lax.broadcasted_iota(jnp.int32, (1344, 384), 0)
    col = lax.broadcasted_iota(jnp.int32, (1, 384), 1)
    r = lax.rem(col, 24)
    for block in range(4):
        want = jnp.where(r < 21, (col // 24) * 84 + block * 21 + r, -1)
        order = jnp.where(source == want, 1.0, 0.0).astype(BF16)
        y = jnp.dot(h_ref[...], order, preferred_element_type=F32).astype(BF16)
        store(y, (block,), 1024)
    copies[3].wait()
    for k in range(8):
        width = 512 if k < 7 else 448
        store(piece(q_ref[:, 512 * k:512 * k + width]), (k // 2,), 512 * (k % 2))
    for slot in range(4):
        for ref in (keep_ref, give_ref):
            ref[4 * slot + 3, :, 960:1024] = jnp.zeros((24, 64), BF16)


VMEM = pl.BlockSpec(memory_space=pltpu.VMEM)
HBM = pl.BlockSpec(memory_space=pltpu.HBM)


def contract(coeffs, q, p, w_in, w_out):
    shape = jax.ShapeDtypeStruct((16, 24, 1536), BF16)
    return pl.pallas_call(
        contract_kernel,
        out_shape=(shape, shape),
        in_specs=[HBM] * 5,
        out_specs=(VMEM, VMEM),
        scratch_shapes=[pltpu.VMEM((168, 4032), F32), pltpu.VMEM((168, 1344), F32),
                        pltpu.VMEM((168, 64), F32), pltpu.VMEM((168, 64), F32),
                        pltpu.VMEM((192, 1344), BF16), pltpu.VMEM((8, 8), F32),
                        pltpu.SemaphoreType.DMA((5,))],
        name="contract",
        compiler_params=pltpu.CompilerParams(vmem_limit_bytes=16 << 20),
        cost_estimate=pl.CostEstimate(flops=3 * 2 * 192 * 168 * 5504, bytes_accessed=6000000,
                                      transcendentals=0),
    )(*[pltpu.with_memory_space_constraint(x, pltpu.HBM) for x in (coeffs, q, p, w_in, w_out)])


def pair_kernel(a_ref, b_ref, o_ref):
    for k in range(16):
        o_ref[k] = (a_ref[k].astype(F32) + b_ref[k].astype(F32)).astype(BF16)


def pair_sum(a, b):
    return pl.pallas_call(
        pair_kernel,
        out_shape=jax.ShapeDtypeStruct((16, 24, 1536), BF16),
        name="pair",
        compiler_params=pltpu.CompilerParams(vmem_limit_bytes=8 << 20),
        cost_estimate=pl.CostEstimate(flops=600000, bytes_accessed=3600000, transcendentals=0),
    )(a, b)


def lines(values, count, width):
    hi = values.astype(BF16).astype(F32)
    lo = values - hi
    parts = [x[:, width * k:width * k + width] for x in (hi, lo) for k in range(count)]
    row = lax.broadcasted_iota(jnp.int32, (8, width), 0)
    out = jnp.zeros((8, width), F32)
    for k, part in enumerate(parts):
        out = jnp.where(row == k, part, out)
    return out


def unlines(rows, count):
    return jnp.concatenate([rows[k:k + 1] + rows[count + k:count + k + 1] for k in range(count)],
                           axis=1)


def partial_kernel(g_ref, o_ref, p_ref):
    total = (g_ref[0:8].astype(F32) + g_ref[8:16].astype(F32)).reshape(192, 1536)
    w_in = total[:, 1408:1472]
    norm = jnp.sqrt(jnp.sum(w_in * w_in, axis=1, keepdims=True))
    w_in = (w_in / (EPS + norm)).astype(BF16)
    w_out = total[:, 1472:1536].astype(BF16)
    n = lax.dot_general(w_in, w_out, TN, preferred_element_type=F32)
    proj = total[:, 1024:1408]
    p_ref[...] = proj
    y = lax.axis_index("y")
    own = [g_ref[4 * x + y].astype(F32) + g_ref[8 + 4 * x + y].astype(F32) for x in range(2)]
    own = jnp.concatenate([x[:, 1472:1536] for x in own], axis=1)
    low = jnp.concatenate([own, lines(jnp.sum(proj * proj, axis=0, keepdims=True), 3, 128)], axis=0)
    for z in range(8):
        q = total[:, 128 * z:128 * z + 128]
        m = lax.dot_general(w_in, q.astype(BF16), TN, preferred_element_type=F32)
        side = lines(jnp.sum(q * q, axis=0, keepdims=True), 2, 64)
        tail = jnp.concatenate([n[8 * z:8 * z + 8], side], axis=1)
        o_ref[z] = jnp.concatenate([m, tail, low], axis=0).astype(BF16)


def partial_products(got):
    return pl.pallas_call(
        partial_kernel,
        out_shape=(jax.ShapeDtypeStruct((8, 104, 128), BF16),
                   jax.ShapeDtypeStruct((192, 384), F32)),
        name="partial",
        compiler_params=pltpu.CompilerParams(vmem_limit_bytes=8 << 20),
        cost_estimate=pl.CostEstimate(flops=2 * 64 * 192 * 1152, bytes_accessed=1000000,
                                      transcendentals=0),
    )(got)


def whole_kernel(g_ref, p_ref, o_ref, r_ref):
    total = g_ref[0].astype(F32)
    for z in range(1, 8):
        total = total + g_ref[z].astype(F32)
    m = total[0:64] / (EPS + jnp.sqrt(unlines(total[64:72, 64:128], 2)))
    out = jnp.concatenate([m, total[64:72]], axis=0).astype(BF16)
    for k in range(32):
        o_ref[k] = out
    w_out = g_ref[:, 72:96, :].astype(F32).reshape(192, 128)
    w_out = jnp.concatenate([w_out[:, :64], w_out[:, 64:]], axis=0)
    norm = jnp.sqrt(unlines(total[96:104], 3))
    proj = (p_ref[...] / (EPS + norm)).astype(BF16)
    r = jnp.dot(proj, w_out.astype(BF16), preferred_element_type=F32)
    square = lines(jnp.sum(w_out * w_out, axis=0, keepdims=True), 1, 64)
    square = jnp.concatenate([square, square], axis=1)
    mine = lax.axis_index("y")
    for y in range(4):
        both = jnp.concatenate([r[24 * y:24 * y + 24], r[96 + 24 * y:120 + 24 * y]], axis=1)
        r_ref[lax.rem(y + 4 - mine, 4)] = jnp.concatenate([both, square], axis=0).astype(BF16)


def whole_products(got, proj):
    return pl.pallas_call(
        whole_kernel,
        out_shape=(jax.ShapeDtypeStruct((32, 72, 128), BF16),
                   jax.ShapeDtypeStruct((4, 32, 128), BF16)),
        name="whole",
        compiler_params=pltpu.CompilerParams(vmem_limit_bytes=8 << 20),
        cost_estimate=pl.CostEstimate(flops=100000, bytes_accessed=800000, transcendentals=0),
    )(got, proj)


def attend_kernel(t_ref, b_ref, a_ref, s_ref, e_ref, d_ref):
    tokens = jnp.concatenate([t_ref[0], t_ref[1]], axis=1)

    def project(g, carry):
        xs = []
        for k in range(4):
            x = lax.dot_general(b_ref[4 * g + k, 0:64, :], tokens, TN, preferred_element_type=F32)
            xs.append(x.reshape(2, 64, 512))
        squares = [jnp.sum(x * x, axis=1) for x in xs]
        scale = jnp.sqrt(jnp.concatenate(squares, axis=0) * (1.0 / 64))
        scale = 1.0 / (EPS + scale)
        for k in range(4):
            for half in range(2):
                unit = 16 * k + 2 * g + half
                s_ref[unit] = (xs[k][half] * scale[2 * k + half:2 * k + half + 1]).astype(BF16)
        return carry

    lax.fori_loop(0, 8, project, 0)

    def weigh(h, b, slot):
        at = slice(256 * b, 256 * b + 256)
        scores = lax.dot_general(s_ref[21 + h, :, at], s_ref[h, :, at], TN,
                                 preferred_element_type=F32)
        expo = jnp.exp2(scores * (0.125 * LOG2E))
        e_ref[slot] = expo.astype(BF16)
        d_ref[slot] = jnp.sum(expo.reshape(32, 8, 256), axis=0)

    def gather(h, b, slot):
        at = slice(256 * b, 256 * b + 256)
        out = jnp.dot(s_ref[42 + h, :, at], e_ref[slot], preferred_element_type=F32)
        total = jnp.sum(d_ref[slot], axis=0, keepdims=True)
        a_ref[pl.ds(pl.multiple_of(h * 64, 64), 64), at] = (out * (1.0 / total)).astype(BF16)

    weigh(0, 0, 0)

    def head(h, carry):
        weigh(h, 1, 1)
        gather(h, 0, 0)
        weigh(jnp.minimum(h + 1, 20), 0, 0)
        gather(h, 1, 1)
        return carry

    lax.fori_loop(0, 21, head, 0, unroll=1)


def attend(tokens, got):
    return pl.pallas_call(
        attend_kernel,
        out_shape=jax.ShapeDtypeStruct((1344, 512), BF16),
        scratch_shapes=[pltpu.VMEM((64, 64, 512), BF16), pltpu.VMEM((2, 256, 256), BF16),
                        pltpu.VMEM((2, 8, 256), F32)],
        name="attend",
        compiler_params=pltpu.CompilerParams(vmem_limit_bytes=16 << 20),
        cost_estimate=pl.CostEstimate(flops=5000000000, bytes_accessed=2400000, transcendentals=2800000),
    )(tokens, got)


def output_kernel(t_ref, b_ref, a_ref, r_ref, s_out_ref, own_ref, other_ref, z_ref):
    tokens = jnp.concatenate([t_ref[0], t_ref[1]], axis=1)
    feature = 0.3 * lax.dot_general(r_ref[...], a_ref[...], TN, preferred_element_type=F32)
    n = jnp.concatenate([b_ref[4 * z, 64:72, 0:64].astype(F32) for z in range(8)], axis=0)
    feature = feature + 0.7 * lax.dot_general(n.astype(BF16), tokens, TN, preferred_element_type=F32)
    feature = feature * (s_out_ref[...] * (1.0 / (0.58 ** 0.5)))
    token = lax.broadcasted_iota(jnp.int32, (256, 256), 0)
    lane = lax.broadcasted_iota(jnp.int32, (256, 256), 1)
    keep = lax.rem(token, 16) == lane // 16
    row = lax.broadcasted_iota(jnp.int32, (128, 256), 0)
    lane = lax.broadcasted_iota(jnp.int32, (128, 256), 1)
    for b in range(2):
        part = feature[:, 256 * b:256 * b + 256]
        hi = part.astype(BF16)
        lo = (part - hi.astype(F32)).astype(BF16)
        both = jnp.concatenate([hi, lo], axis=0)
        for i in range(4):
            tile = jnp.where(lax.rem(row, 64) == 16 * i + lax.rem(lane, 16), 1.0, 0.0).astype(BF16)
            wide = lax.dot_general(both, tile, TN, preferred_element_type=F32)
            wide = jnp.where(keep, wide, 0.0).reshape(16, 16, 256)
            wide = jnp.sum(wide, axis=1)
            z_ref[2 * b, pl.ds(i, 16, stride=4), :] = wide[:, :128]
            z_ref[2 * b + 1, pl.ds(i, 16, stride=4), :] = wide[:, 128:]
    mine = lax.axis_index("xl")
    for ref, b in ((own_ref, mine), (other_ref, 1 - mine)):
        ref[...] = jnp.concatenate([z_ref[2 * b], z_ref[2 * b + 1]], axis=1)


def output(tokens, got, attended, r, scale):
    return pl.pallas_call(
        output_kernel,
        out_shape=(jax.ShapeDtypeStruct((64, 256), F32),) * 2,
        scratch_shapes=[pltpu.VMEM((4, 64, 128), F32)],
        name="output",
        compiler_params=pltpu.CompilerParams(vmem_limit_bytes=12 << 20),
        cost_estimate=pl.CostEstimate(flops=100000000, bytes_accessed=2000000, transcendentals=0),
    )(tokens, got, attended, r, scale)


def shards(snap_in, snap_qkv, snap_proj, snap_out, coeffs, latent, levels):
    swap = [(0, 1), (1, 0)]
    keep, give = contract(
        coeffs,
        snap_qkv.transpose(1, 0, 2).reshape(168, 4032),
        snap_proj.transpose(1, 0, 2).reshape(168, 1344),
        snap_in.transpose(2, 0, 1).reshape(168, 64),
        snap_out.transpose(1, 0, 2).reshape(168, 64),
    )
    part = pair_sum(keep, lax.ppermute(give, "core", swap))
    part = a2a(part, ("xh", "xl", "y"))
    send, proj = partial_products(part)
    send, side = whole_products(a2a(send, "z"), proj)
    send, latent, levels = lax.optimization_barrier((send, latent, levels))
    got = a2a(send, ZY)

    total = side[0].astype(F32)
    for d in range(1, 4):
        total = total + lax.ppermute(side[d], "y", [(k, (k + d) % 4) for k in range(4)]).astype(F32)
    scale = 1.0 / (EPS + jnp.sqrt(total[24, :64] + total[25, :64]))
    r = jnp.broadcast_to(total[None, :24].astype(BF16), (32, 24, 128))
    r, _ = lax.optimization_barrier((r, got))
    r = a2a(r, ZY)[:, :21]
    r = jnp.concatenate([r[:, :, :64], r[:, :, 64:]], axis=0).reshape(1344, 64)

    c_in, c_skip, c_out = noise_scales(levels)
    tokens = (c_in[:, None, None] * latent).astype(BF16)
    tokens = tokens.reshape(16, 4, 16, 16).transpose(1, 3, 0, 2).reshape(1, 64, 256)
    tokens = lax.all_gather(tokens, "xl", axis=0, tiled=True)
    attended = attend(tokens, got)
    own, other = output(tokens, got, attended, r, scale[:, None])
    other = lax.ppermute(other, "xl", swap)
    first = lax.axis_index("xl") == 0
    feature = jnp.stack([jnp.where(first, own, other), jnp.where(first, other, own)])
    out = c_skip[:, None, None] * latent + c_out[:, None, None] * feature
    return out[:, None]


def solution(mesh):
    fine = Mesh(mesh.devices.reshape(2, 2, 2, 8, 4), ("xh", "core", "xl", "z", "y"))
    in_specs = (
        P(SNAP, None, PARAM),
        P(SNAP, PARAM, None),
        P(SNAP, PARAM, None),
        P(SNAP, PARAM, None),
        P(SNAP, None),
        P(PARAM, None, None),
        P(PARAM),
    )
    out_specs = P(SNAP, PARAM, None, None)
    return jax.shard_map(shards, mesh=fine, in_specs=in_specs, out_specs=out_specs, check_vma=False)
```

```python
import jax
import jax.numpy as jnp
from jax import lax
from jax.experimental import pallas as pl
from jax.experimental.pallas import tpu as pltpu
from jax.sharding import Mesh, PartitionSpec as P

HEAD_DIM = 64
PROF = 8
NLEV = 16
EPS = 0.0001
LOG2E = 1.4426950408889634

SNAP = ("xh", "core")
PARAM = ("xl", "z", "y")
ZY = ("z", "y")
X = ("xh", "xl")
F32 = jnp.float32
BF16 = jnp.bfloat16
TN = (((0,), (0,)), ((), ()))


def noise_scales(levels):
    step = levels.astype(jnp.float32) / (NLEV - 1)
    sigma = jnp.exp(jnp.log(0.2) + step * (jnp.log(5.0) - jnp.log(0.2)))
    square = sigma * sigma + 0.25
    return (1.0 / jnp.sqrt(square), 0.25 / square, 0.5 * sigma / jnp.sqrt(square))


def a2a(x, axis):
    return lax.all_to_all(x, axis, 0, 0, tiled=True)


def contract_kernel(c_hbm, q_hbm, p_hbm, i_hbm, o_hbm, keep_ref, give_ref, q_ref, p_ref, i_ref,
                    o_ref, h_ref, c_ref, sems):
    pairs = [(c_hbm, c_ref), (i_hbm, i_ref), (o_hbm, o_ref), (p_hbm, p_ref), (q_hbm, q_ref)]
    copies = [pltpu.make_async_copy(a, b, sems.at[k]) for k, (a, b) in enumerate(pairs)]
    for copy in copies:
        copy.start()
    copies[0].wait()
    snap = lax.broadcasted_iota(jnp.int32, (8, 168), 0)
    col = lax.broadcasted_iota(jnp.int32, (8, 168), 1)
    pick = jnp.where(lax.rem(col, 8) == snap, 1.0, 0.0)
    rows = lax.dot_general(c_ref[...], pick, TN, precision=lax.Precision.HIGHEST,
                           preferred_element_type=F32)
    r = lax.broadcasted_iota(jnp.int32, (24, 168), 0)
    col = lax.broadcasted_iota(jnp.int32, (24, 168), 1)
    same = jnp.where(col // 8 == r, 1.0, 0.0)
    mine = lax.axis_index("core")
    picked = []
    for k in range(2):
        for slot in range(4):
            p = (slot // 2) * 4 + slot % 2
            picked.append(jnp.where(mine == k, rows[p:p + 1], rows[p + 2:p + 3]))
    mix = jnp.concatenate([row * same for row in picked], axis=0)
    mix_hi = mix.astype(BF16)
    mix_lo = (mix - mix_hi.astype(F32)).astype(BF16)

    def piece(x):
        hi = x.astype(BF16)
        lo = (x - hi.astype(F32)).astype(BF16)
        y = jnp.dot(mix_hi, hi, preferred_element_type=F32)
        y = y + jnp.dot(mix_hi, lo, preferred_element_type=F32)
        y = y + jnp.dot(mix_lo, hi, preferred_element_type=F32)
        return y.astype(BF16)

    def store(y, blocks, at):
        width = y.shape[1]
        for k, ref in enumerate((keep_ref, give_ref)):
            for slot in range(4):
                row = 96 * k + 24 * slot
                for block in blocks:
                    ref[4 * slot + block, :, at:at + width] = y[row:row + 24]

    copies[1].wait()
    copies[2].wait()
    store(piece(jnp.concatenate([i_ref[...], o_ref[...]], axis=1)), range(4), 1408)
    copies[3].wait()
    for start, width in ((0, 512), (512, 512), (1024, 320)):
        h_ref[:, start:start + width] = piece(p_ref[:, start:start + width])
    source = lax.broadcasted_iota(jnp.int32, (1344, 384), 0)
    col = lax.broadcasted_iota(jnp.int32, (1, 384), 1)
    r = lax.rem(col, 24)
    for block in range(4):
        want = jnp.where(r < 21, (col // 24) * 84 + block * 21 + r, -1)
        order = jnp.where(source == want, 1.0, 0.0).astype(BF16)
        y = jnp.dot(h_ref[...], order, preferred_element_type=F32).astype(BF16)
        store(y, (block,), 1024)
    for k in range(8):
        if k == 0:
            copies[4].wait()
        width = 512 if k < 7 else 448
        store(piece(q_ref[:, 512 * k:512 * k + width]), (k // 2,), 512 * (k % 2))
    for slot in range(4):
        for ref in (keep_ref, give_ref):
            ref[4 * slot + 3, :, 960:1024] = jnp.zeros((24, 64), BF16)


VMEM = pl.BlockSpec(memory_space=pltpu.VMEM)
HBM = pl.BlockSpec(memory_space=pltpu.HBM)


def contract(coeffs, q, p, w_in, w_out):
    shape = jax.ShapeDtypeStruct((16, 24, 1536), BF16)
    return pl.pallas_call(
        contract_kernel,
        out_shape=(shape, shape),
        in_specs=[HBM] * 5,
        out_specs=(VMEM, VMEM),
        scratch_shapes=[pltpu.VMEM((168, 4032), F32), pltpu.VMEM((168, 1344), F32),
                        pltpu.VMEM((168, 64), F32), pltpu.VMEM((168, 64), F32),
                        pltpu.VMEM((192, 1344), BF16), pltpu.VMEM((8, 8), F32),
                        pltpu.SemaphoreType.DMA((5,))],
        name="contract",
        compiler_params=pltpu.CompilerParams(vmem_limit_bytes=16 << 20),
        cost_estimate=pl.CostEstimate(flops=3 * 2 * 192 * 168 * 5504, bytes_accessed=6000000,
                                      transcendentals=0),
    )(*[pltpu.with_memory_space_constraint(x, pltpu.HBM) for x in (coeffs, q, p, w_in, w_out)])


def pair_kernel(a_ref, b_ref, o_ref):
    for k in range(16):
        o_ref[k] = (a_ref[k].astype(F32) + b_ref[k].astype(F32)).astype(BF16)


def pair_sum(a, b):
    return pl.pallas_call(
        pair_kernel,
        out_shape=jax.ShapeDtypeStruct((16, 24, 1536), BF16),
        name="pair",
        compiler_params=pltpu.CompilerParams(vmem_limit_bytes=8 << 20),
        cost_estimate=pl.CostEstimate(flops=600000, bytes_accessed=3600000, transcendentals=0),
    )(a, b)


def lines(values, count, width):
    hi = values.astype(BF16).astype(F32)
    lo = values - hi
    parts = [x[:, width * k:width * k + width] for x in (hi, lo) for k in range(count)]
    row = lax.broadcasted_iota(jnp.int32, (8, width), 0)
    out = jnp.zeros((8, width), F32)
    for k, part in enumerate(parts):
        out = jnp.where(row == k, part, out)
    return out


def unlines(rows, count):
    return jnp.concatenate([rows[k:k + 1] + rows[count + k:count + k + 1] for k in range(count)],
                           axis=1)


def partial_kernel(g_ref, o_ref, p_ref):
    total = (g_ref[0:8].astype(F32) + g_ref[8:16].astype(F32)).reshape(192, 1536)
    w_in = total[:, 1408:1472]
    norm = jnp.sqrt(jnp.sum(w_in * w_in, axis=1, keepdims=True))
    w_in = (w_in / (EPS + norm)).astype(BF16)
    w_out = total[:, 1472:1536].astype(BF16)
    n = lax.dot_general(w_in, w_out, TN, preferred_element_type=F32)
    proj = total[:, 1024:1408]
    p_ref[...] = proj
    y = lax.axis_index("y")
    own = [g_ref[4 * x + y].astype(F32) + g_ref[8 + 4 * x + y].astype(F32) for x in range(2)]
    own = jnp.concatenate([x[:, 1472:1536] for x in own], axis=1)
    low = jnp.concatenate([own, lines(jnp.sum(proj * proj, axis=0, keepdims=True), 3, 128)], axis=0)
    for z in range(8):
        q = total[:, 128 * z:128 * z + 128]
        m = lax.dot_general(w_in, q.astype(BF16), TN, preferred_element_type=F32)
        side = lines(jnp.sum(q * q, axis=0, keepdims=True), 2, 64)
        tail = jnp.concatenate([n[8 * z:8 * z + 8], side], axis=1)
        o_ref[z] = jnp.concatenate([m, tail, low], axis=0).astype(BF16)


def partial_products(got):
    return pl.pallas_call(
        partial_kernel,
        out_shape=(jax.ShapeDtypeStruct((8, 104, 128), BF16),
                   jax.ShapeDtypeStruct((192, 384), F32)),
        name="partial",
        compiler_params=pltpu.CompilerParams(vmem_limit_bytes=8 << 20),
        cost_estimate=pl.CostEstimate(flops=2 * 64 * 192 * 1152, bytes_accessed=1000000,
                                      transcendentals=0),
    )(got)


def whole_kernel(g_ref, p_ref, o_ref, r_ref, n_ref):
    total = g_ref[0].astype(F32)
    for z in range(1, 8):
        total = total + g_ref[z].astype(F32)
    m = total[0:64] / (EPS + jnp.sqrt(unlines(total[64:72, 64:128], 2)))
    n_ref[...] = total[64:72]
    out = m.astype(BF16)
    for k in range(32):
        o_ref[k] = out
    w_out = g_ref[:, 72:96, :].astype(F32).reshape(192, 128)
    w_out = jnp.concatenate([w_out[:, :64], w_out[:, 64:]], axis=0)
    norm = jnp.sqrt(unlines(total[96:104], 3))
    proj = (p_ref[...] / (EPS + norm)).astype(BF16)
    r = jnp.dot(proj, w_out.astype(BF16), preferred_element_type=F32)
    square = lines(jnp.sum(w_out * w_out, axis=0, keepdims=True), 1, 64)
    square = jnp.concatenate([square, square], axis=1)
    mine = lax.axis_index("y")
    for y in range(4):
        both = jnp.concatenate([r[24 * y:24 * y + 24], r[96 + 24 * y:120 + 24 * y]], axis=1)
        r_ref[lax.rem(y + 4 - mine, 4)] = jnp.concatenate([both, square], axis=0).astype(BF16)


def whole_products(got, proj):
    return pl.pallas_call(
        whole_kernel,
        out_shape=(jax.ShapeDtypeStruct((32, 64, 128), BF16),
                   jax.ShapeDtypeStruct((4, 32, 128), BF16),
                   jax.ShapeDtypeStruct((8, 128), F32)),
        name="whole",
        compiler_params=pltpu.CompilerParams(vmem_limit_bytes=8 << 20),
        cost_estimate=pl.CostEstimate(flops=100000, bytes_accessed=800000, transcendentals=0),
    )(got, proj)


def spread_kernel(a_ref, b_ref, c_ref, d_ref, n_ref, o_ref):
    total = a_ref[0].astype(F32)
    for ref in (b_ref, c_ref, d_ref):
        total = total + ref[...].astype(F32)
    scale = 1.0 / (EPS + jnp.sqrt(total[24:25] + total[25:26]))
    out = jnp.concatenate([total[:24] * scale, n_ref[...] * scale], axis=0).astype(BF16)
    for k in range(32):
        o_ref[k] = out


def spread(side, parts, n):
    return pl.pallas_call(
        spread_kernel,
        out_shape=jax.ShapeDtypeStruct((32, 32, 128), BF16),
        name="spread",
        compiler_params=pltpu.CompilerParams(vmem_limit_bytes=4 << 20),
        cost_estimate=pl.CostEstimate(flops=20000, bytes_accessed=300000, transcendentals=0),
    )(side, *parts, n)


def attend_kernel(t_ref, u_ref, b_ref, a_ref, s_ref, e_ref, d_ref):
    tokens = jnp.concatenate([t_ref[...], u_ref[...]], axis=1)

    def project(g, carry):
        xs = []
        for k in range(4):
            x = lax.dot_general(b_ref[4 * g + k, 0:64, :], tokens, TN, preferred_element_type=F32)
            xs.append(x.reshape(2, 64, 512))
        squares = [jnp.sum(x * x, axis=1) for x in xs]
        scale = jnp.sqrt(jnp.concatenate(squares, axis=0) * (1.0 / 64))
        scale = 1.0 / (EPS + scale)
        for k in range(4):
            for half in range(2):
                unit = 16 * k + 2 * g + half
                s_ref[unit] = (xs[k][half] * scale[2 * k + half:2 * k + half + 1]).astype(BF16)
        return carry

    lax.fori_loop(0, 8, project, 0)

    def weigh(h, b, slot):
        at = slice(256 * b, 256 * b + 256)
        scores = lax.dot_general(s_ref[21 + h, :, at], s_ref[h, :, at], TN,
                                 preferred_element_type=F32)
        expo = jnp.exp2(scores * (0.125 * LOG2E))
        e_ref[slot] = expo.astype(BF16)
        d_ref[slot] = jnp.sum(expo.reshape(32, 8, 256), axis=0)

    def gather(h, b, slot):
        at = slice(256 * b, 256 * b + 256)
        out = jnp.dot(s_ref[42 + h, :, at], e_ref[slot], preferred_element_type=F32)
        total = jnp.sum(d_ref[slot], axis=0, keepdims=True)
        a_ref[pl.ds(pl.multiple_of(h * 64, 64), 64), at] = (out * (1.0 / total)).astype(BF16)

    weigh(0, 0, 0)

    def head(h, carry):
        weigh(h, 1, 1)
        gather(h, 0, 0)
        weigh(jnp.minimum(h + 1, 20), 0, 0)
        gather(h, 1, 1)
        return carry

    lax.fori_loop(0, 21, head, 0, unroll=1)


def attend(tokens, others, got):
    return pl.pallas_call(
        attend_kernel,
        out_shape=jax.ShapeDtypeStruct((1344, 512), BF16),
        scratch_shapes=[pltpu.VMEM((64, 64, 512), BF16), pltpu.VMEM((2, 256, 256), BF16),
                        pltpu.VMEM((2, 8, 256), F32)],
        name="attend",
        compiler_params=pltpu.CompilerParams(vmem_limit_bytes=16 << 20),
        cost_estimate=pl.CostEstimate(flops=5000000000, bytes_accessed=2400000, transcendentals=2800000),
    )(tokens, others, got)


def output_kernel(t_ref, u_ref, a_ref, r_ref, n_ref, own_ref, other_ref, z_ref):
    tokens = jnp.concatenate([t_ref[...], u_ref[...]], axis=1)
    feature = 0.3 * lax.dot_general(r_ref[...], a_ref[...], TN, preferred_element_type=F32)
    feature = feature + 0.7 * lax.dot_general(n_ref[...], tokens, TN, preferred_element_type=F32)
    feature = feature * (1.0 / (0.58 ** 0.5))
    token = lax.broadcasted_iota(jnp.int32, (256, 256), 0)
    lane = lax.broadcasted_iota(jnp.int32, (256, 256), 1)
    keep = lax.rem(token, 16) == lane // 16
    row = lax.broadcasted_iota(jnp.int32, (128, 256), 0)
    lane = lax.broadcasted_iota(jnp.int32, (128, 256), 1)
    for b in range(2):
        part = feature[:, 256 * b:256 * b + 256]
        hi = part.astype(BF16)
        lo = (part - hi.astype(F32)).astype(BF16)
        both = jnp.concatenate([hi, lo], axis=0)
        for i in range(4):
            tile = jnp.where(lax.rem(row, 64) == 16 * i + lax.rem(lane, 16), 1.0, 0.0).astype(BF16)
            wide = lax.dot_general(both, tile, TN, preferred_element_type=F32)
            wide = jnp.where(keep, wide, 0.0).reshape(16, 16, 256)
            wide = jnp.sum(wide, axis=1)
            z_ref[2 * b, pl.ds(i, 16, stride=4), :] = wide[:, :128]
            z_ref[2 * b + 1, pl.ds(i, 16, stride=4), :] = wide[:, 128:]
    own_ref[...] = jnp.concatenate([z_ref[0], z_ref[1]], axis=1)
    other_ref[...] = jnp.concatenate([z_ref[2], z_ref[3]], axis=1).astype(BF16)


def output(tokens, others, attended, r, n):
    return pl.pallas_call(
        output_kernel,
        out_shape=(jax.ShapeDtypeStruct((64, 256), F32), jax.ShapeDtypeStruct((64, 256), BF16)),
        scratch_shapes=[pltpu.VMEM((4, 64, 128), F32)],
        name="output",
        compiler_params=pltpu.CompilerParams(vmem_limit_bytes=12 << 20),
        cost_estimate=pl.CostEstimate(flops=100000000, bytes_accessed=2000000, transcendentals=0),
    )(tokens, others, attended, r, n)


def shards(snap_in, snap_qkv, snap_proj, snap_out, coeffs, latent, levels):
    swap = [(0, 1), (1, 0)]
    keep, give = contract(
        coeffs,
        snap_qkv.transpose(1, 0, 2).reshape(168, 4032),
        snap_proj.transpose(1, 0, 2).reshape(168, 1344),
        snap_in.transpose(2, 0, 1).reshape(168, 64),
        snap_out.transpose(1, 0, 2).reshape(168, 64),
    )
    part = pair_sum(keep, lax.ppermute(give, "core", swap))
    part = a2a(part, ("xh", "xl", "y"))
    send, proj = partial_products(part)
    send, side, n = whole_products(a2a(send, "z"), proj)
    send, latent, levels = lax.optimization_barrier((send, latent, levels))
    got = a2a(send, ZY)

    c_in, c_skip, c_out = noise_scales(levels)
    tokens = (c_in[:, None, None] * latent).astype(BF16)
    tokens = tokens.reshape(16, 4, 16, 16).transpose(1, 3, 0, 2).reshape(64, 256)
    others = lax.ppermute(tokens, "xl", swap)
    parts = [lax.ppermute(side[d], "y", [(k, (k + d) % 4) for k in range(4)]) for d in range(1, 4)]
    r = spread(side, parts, n)
    r, others, _ = lax.optimization_barrier((r, others, got))
    r = a2a(r, ZY)
    n = r.reshape(8, 4, 32, 128)[:, 0, 24:, :64].reshape(64, 64)
    r = jnp.concatenate([r[:, :21, :64], r[:, :21, 64:]], axis=0).reshape(1344, 64)

    attended = attend(tokens, others, got)
    own, other = output(tokens, others, attended, r, n)
    other = lax.ppermute(other, "xl", swap).astype(F32)
    first = lax.axis_index("xl") == 0
    feature = jnp.stack([jnp.where(first, own, other), jnp.where(first, other, own)])
    out = c_skip[:, None, None] * latent + c_out[:, None, None] * feature
    return out[:, None]


def solution(mesh):
    fine = Mesh(mesh.devices.reshape(2, 2, 2, 8, 4), ("xh", "core", "xl", "z", "y"))
    in_specs = (
        P(SNAP, None, PARAM),
        P(SNAP, PARAM, None),
        P(SNAP, PARAM, None),
        P(SNAP, PARAM, None),
        P(SNAP, None),
        P(PARAM, None, None),
        P(PARAM),
    )
    out_specs = P(SNAP, PARAM, None, None)
    return jax.shard_map(shards, mesh=fine, in_specs=in_specs, out_specs=out_specs, check_vma=False)
```

```python
import jax
import jax.numpy as jnp
from jax import lax
from jax.experimental import pallas as pl
from jax.experimental.pallas import tpu as pltpu
from jax.sharding import Mesh, PartitionSpec as P

HEAD_DIM = 64
PROF = 8
NLEV = 16
EPS = 0.0001
LOG2E = 1.4426950408889634

SNAP = ("xh", "core")
PARAM = ("xl", "z", "y")
ZY = ("z", "y")
X = ("xh", "xl")
F32 = jnp.float32
BF16 = jnp.bfloat16
TN = (((0,), (0,)), ((), ()))


def noise_scales(levels):
    step = levels.astype(jnp.float32) / (NLEV - 1)
    sigma = jnp.exp(jnp.log(0.2) + step * (jnp.log(5.0) - jnp.log(0.2)))
    square = sigma * sigma + 0.25
    return (1.0 / jnp.sqrt(square), 0.25 / square, 0.5 * sigma / jnp.sqrt(square))


def a2a(x, axis):
    return lax.all_to_all(x, axis, 0, 0, tiled=True)


def contract_kernel(c_hbm, q_hbm, p_hbm, i_hbm, o_hbm, keep_ref, give_ref, q_ref, p_ref, i_ref,
                    o_ref, h_ref, c_ref, sems):
    pairs = [(c_hbm, c_ref), (i_hbm, i_ref), (o_hbm, o_ref), (p_hbm, p_ref), (q_hbm, q_ref)]
    copies = [pltpu.make_async_copy(a, b, sems.at[k]) for k, (a, b) in enumerate(pairs)]
    for copy in copies:
        copy.start()
    copies[0].wait()
    snap = lax.broadcasted_iota(jnp.int32, (8, 168), 0)
    col = lax.broadcasted_iota(jnp.int32, (8, 168), 1)
    pick = jnp.where(lax.rem(col, 8) == snap, 1.0, 0.0)
    rows = lax.dot_general(c_ref[...], pick, TN, precision=lax.Precision.HIGHEST,
                           preferred_element_type=F32)
    r = lax.broadcasted_iota(jnp.int32, (24, 168), 0)
    col = lax.broadcasted_iota(jnp.int32, (24, 168), 1)
    same = jnp.where(col // 8 == r, 1.0, 0.0)
    mine = lax.axis_index("core")
    picked = []
    for k in range(2):
        for slot in range(4):
            p = (slot // 2) * 4 + slot % 2
            picked.append(jnp.where(mine == k, rows[p:p + 1], rows[p + 2:p + 3]))
    mix = jnp.concatenate([row * same for row in picked], axis=0)
    mix_hi = mix.astype(BF16)
    mix_lo = (mix - mix_hi.astype(F32)).astype(BF16)

    def piece(x):
        hi = x.astype(BF16)
        lo = (x - hi.astype(F32)).astype(BF16)
        y = jnp.dot(mix_hi, hi, preferred_element_type=F32)
        y = y + jnp.dot(mix_hi, lo, preferred_element_type=F32)
        y = y + jnp.dot(mix_lo, hi, preferred_element_type=F32)
        return y.astype(BF16)

    def store(y, blocks, at):
        width = y.shape[1]
        for k, ref in enumerate((keep_ref, give_ref)):
            for slot in range(4):
                row = 96 * k + 24 * slot
                for block in blocks:
                    ref[4 * slot + block, :, at:at + width] = y[row:row + 24]

    copies[1].wait()
    copies[2].wait()
    store(piece(jnp.concatenate([i_ref[...], o_ref[...]], axis=1)), range(4), 1408)
    copies[3].wait()
    for start, width in ((0, 512), (512, 512), (1024, 320)):
        h_ref[:, start:start + width] = piece(p_ref[:, start:start + width])
    source = lax.broadcasted_iota(jnp.int32, (1344, 384), 0)
    col = lax.broadcasted_iota(jnp.int32, (1, 384), 1)
    r = lax.rem(col, 24)
    for block in range(4):
        want = jnp.where(r < 21, (col // 24) * 84 + block * 21 + r, -1)
        order = jnp.where(source == want, 1.0, 0.0).astype(BF16)
        y = jnp.dot(h_ref[...], order, preferred_element_type=F32).astype(BF16)
        store(y, (block,), 1024)
    for k in range(8):
        if k == 0:
            copies[4].wait()
        width = 512 if k < 7 else 448
        store(piece(q_ref[:, 512 * k:512 * k + width]), (k // 2,), 512 * (k % 2))
    for slot in range(4):
        for ref in (keep_ref, give_ref):
            ref[4 * slot + 3, :, 960:1024] = jnp.zeros((24, 64), BF16)


VMEM = pl.BlockSpec(memory_space=pltpu.VMEM)
HBM = pl.BlockSpec(memory_space=pltpu.HBM)


def contract(coeffs, q, p, w_in, w_out):
    shape = jax.ShapeDtypeStruct((16, 24, 1536), BF16)
    return pl.pallas_call(
        contract_kernel,
        out_shape=(shape, shape),
        in_specs=[HBM] * 5,
        out_specs=(VMEM, VMEM),
        scratch_shapes=[pltpu.VMEM((168, 4032), F32), pltpu.VMEM((168, 1344), F32),
                        pltpu.VMEM((168, 64), F32), pltpu.VMEM((168, 64), F32),
                        pltpu.VMEM((192, 1344), BF16), pltpu.VMEM((8, 8), F32),
                        pltpu.SemaphoreType.DMA((5,))],
        name="contract",
        compiler_params=pltpu.CompilerParams(vmem_limit_bytes=16 << 20),
        cost_estimate=pl.CostEstimate(flops=3 * 2 * 192 * 168 * 5504, bytes_accessed=6000000,
                                      transcendentals=0),
    )(*[pltpu.with_memory_space_constraint(x, pltpu.HBM) for x in (coeffs, q, p, w_in, w_out)])


def pair_kernel(a_ref, b_ref, o_ref):
    for k in range(16):
        o_ref[k] = (a_ref[k].astype(F32) + b_ref[k].astype(F32)).astype(BF16)


def pair_sum(a, b):
    return pl.pallas_call(
        pair_kernel,
        out_shape=jax.ShapeDtypeStruct((16, 24, 1536), BF16),
        name="pair",
        compiler_params=pltpu.CompilerParams(vmem_limit_bytes=8 << 20),
        cost_estimate=pl.CostEstimate(flops=600000, bytes_accessed=3600000, transcendentals=0),
    )(a, b)


def lines(values, count, width):
    hi = values.astype(BF16).astype(F32)
    lo = values - hi
    parts = [x[:, width * k:width * k + width] for x in (hi, lo) for k in range(count)]
    row = lax.broadcasted_iota(jnp.int32, (8, width), 0)
    out = jnp.zeros((8, width), F32)
    for k, part in enumerate(parts):
        out = jnp.where(row == k, part, out)
    return out


def unlines(rows, count):
    return jnp.concatenate([rows[k:k + 1] + rows[count + k:count + k + 1] for k in range(count)],
                           axis=1)


def partial_kernel(g_ref, o_ref, p_ref):
    total = (g_ref[0:8].astype(F32) + g_ref[8:16].astype(F32)).reshape(192, 1536)
    w_in = total[:, 1408:1472]
    norm = jnp.sqrt(jnp.sum(w_in * w_in, axis=1, keepdims=True))
    w_in = (w_in / (EPS + norm)).astype(BF16)
    w_out = total[:, 1472:1536].astype(BF16)
    n = lax.dot_general(w_in, w_out, TN, preferred_element_type=F32)
    proj = total[:, 1024:1408]
    p_ref[...] = proj
    y = lax.axis_index("y")
    own = [g_ref[4 * x + y].astype(F32) + g_ref[8 + 4 * x + y].astype(F32) for x in range(2)]
    own = jnp.concatenate([x[:, 1472:1536] for x in own], axis=1)
    low = jnp.concatenate([own, lines(jnp.sum(proj * proj, axis=0, keepdims=True), 3, 128)], axis=0)
    for z in range(8):
        q = total[:, 128 * z:128 * z + 128]
        m = lax.dot_general(w_in, q.astype(BF16), TN, preferred_element_type=F32)
        side = lines(jnp.sum(q * q, axis=0, keepdims=True), 2, 64)
        tail = jnp.concatenate([n[8 * z:8 * z + 8], side], axis=1)
        o_ref[z] = jnp.concatenate([m, tail, low], axis=0).astype(BF16)


def partial_products(got):
    return pl.pallas_call(
        partial_kernel,
        out_shape=(jax.ShapeDtypeStruct((8, 104, 128), BF16),
                   jax.ShapeDtypeStruct((192, 384), F32)),
        name="partial",
        compiler_params=pltpu.CompilerParams(vmem_limit_bytes=8 << 20),
        cost_estimate=pl.CostEstimate(flops=2 * 64 * 192 * 1152, bytes_accessed=1000000,
                                      transcendentals=0),
    )(got)


def whole_kernel(g_ref, p_ref, o_ref, r_ref, n_ref):
    total = g_ref[0].astype(F32)
    for z in range(1, 8):
        total = total + g_ref[z].astype(F32)
    m = total[0:64] / (EPS + jnp.sqrt(unlines(total[64:72, 64:128], 2)))
    n_ref[...] = total[64:72]
    o_ref[...] = m
    w_out = g_ref[:, 72:96, :].astype(F32).reshape(192, 128)
    w_out = jnp.concatenate([w_out[:, :64], w_out[:, 64:]], axis=0)
    norm = jnp.sqrt(unlines(total[96:104], 3))
    proj = (p_ref[...] / (EPS + norm)).astype(BF16)
    r = jnp.dot(proj, w_out.astype(BF16), preferred_element_type=F32)
    square = lines(jnp.sum(w_out * w_out, axis=0, keepdims=True), 1, 64)
    square = jnp.concatenate([square, square], axis=1)
    mine = lax.axis_index("y")
    for y in range(4):
        both = jnp.concatenate([r[24 * y:24 * y + 24], r[96 + 24 * y:120 + 24 * y]], axis=1)
        r_ref[lax.rem(y + 4 - mine, 4)] = jnp.concatenate([both, square], axis=0).astype(BF16)


def whole_products(got, proj):
    return pl.pallas_call(
        whole_kernel,
        out_shape=(jax.ShapeDtypeStruct((64, 128), F32),
                   jax.ShapeDtypeStruct((4, 32, 128), BF16),
                   jax.ShapeDtypeStruct((8, 128), F32)),
        name="whole",
        compiler_params=pltpu.CompilerParams(vmem_limit_bytes=8 << 20),
        cost_estimate=pl.CostEstimate(flops=100000, bytes_accessed=800000, transcendentals=0),
    )(got, proj)


def spread_kernel(a_ref, b_ref, c_ref, d_ref, n_ref, m_ref, o_ref):
    total = a_ref[0].astype(F32)
    for ref in (b_ref, c_ref, d_ref):
        total = total + ref[...].astype(F32)
    scale = 1.0 / (EPS + jnp.sqrt(total[24:25] + total[25:26]))
    n = n_ref[...]
    mine = lax.axis_index("y")
    line = jnp.zeros((1, 128), F32)
    for y in range(4):
        pair = jnp.concatenate([n[2 * y:2 * y + 1, :64], n[2 * y + 1:2 * y + 2, :64]], axis=1)
        line = jnp.where(mine == y, pair, line)
    row = lax.broadcasted_iota(jnp.int32, (24, 128), 0)
    r = jnp.where(row == 21, line, total[:24]) * scale
    out = jnp.concatenate([m_ref[...], r], axis=0).astype(BF16)
    for k in range(32):
        o_ref[k] = out


def spread(side, parts, n, m):
    return pl.pallas_call(
        spread_kernel,
        out_shape=jax.ShapeDtypeStruct((32, 88, 128), BF16),
        name="spread",
        compiler_params=pltpu.CompilerParams(vmem_limit_bytes=4 << 20),
        cost_estimate=pl.CostEstimate(flops=20000, bytes_accessed=800000, transcendentals=0),
    )(side, *parts, n, m)


def attend_kernel(t_ref, u_ref, b_ref, a_ref, s_ref, x0_ref, x1_ref, c0_ref, c1_ref, e0_ref, e1_ref,
                  d0_ref, d1_ref):
    tokens = jnp.concatenate([t_ref[...], u_ref[...]], axis=1)
    blocks, scores, expos, sums = (x0_ref, x1_ref), (c0_ref, c1_ref), (e0_ref, e1_ref), (d0_ref, d1_ref)

    def columns(g, x_ref):
        for k in range(4):
            x = lax.dot_general(b_ref[4 * g + k, 0:64, :], tokens, TN, preferred_element_type=F32)
            x_ref[k] = x.reshape(2, 64, 512)

    def unit(g, x_ref):
        squares = []
        for k in range(4):
            x = x_ref[k]
            squares.append(jnp.sum(x * x, axis=1))
        scale = jnp.sqrt(jnp.concatenate(squares, axis=0) * (1.0 / 64))
        scale = 1.0 / (EPS + scale)
        for k in range(4):
            for half in range(2):
                row = scale[2 * k + half:2 * k + half + 1]
                s_ref[16 * k + 2 * g + half] = (x_ref[k, half] * row).astype(BF16)

    columns(0, x0_ref)
    columns(1, x1_ref)

    def project(i, carry):
        for k in range(2):
            unit(2 * i + k, blocks[k])
            columns(jnp.minimum(2 * i + k + 2, 7), blocks[k])
        return carry

    lax.fori_loop(0, 4, project, 0, unroll=4)

    def score(h, b):
        at = slice(256 * b, 256 * b + 256)
        scores[b][...] = lax.dot_general(s_ref[21 + h, :, at], s_ref[h, :, at], TN,
                                         preferred_element_type=F32)

    def weigh(b):
        expo = jnp.exp2(scores[b][...] * (0.125 * LOG2E))
        expos[b][...] = expo.astype(BF16)
        sums[b][...] = jnp.sum(expo.reshape(32, 8, 256), axis=0)

    def gather(h, b):
        at = slice(256 * b, 256 * b + 256)
        out = jnp.dot(s_ref[42 + h, :, at], expos[b][...], preferred_element_type=F32)
        total = jnp.sum(sums[b][...], axis=0, keepdims=True)
        a_ref[pl.ds(pl.multiple_of(h * 64, 64), 64), at] = (out * (1.0 / total)).astype(BF16)

    score(0, 0)
    score(0, 1)
    e1_ref[...] = jnp.zeros((256, 256), BF16)
    d1_ref[...] = jnp.ones((8, 256), F32)

    def head(h, carry):
        later = jnp.minimum(h + 1, 20)
        weigh(0)
        gather(jnp.maximum(h - 1, 0), 1)
        score(later, 0)
        weigh(1)
        gather(h, 0)
        score(later, 1)
        return carry

    lax.fori_loop(0, 21, head, 0, unroll=21)
    gather(20, 1)


def attend(tokens, others, got):
    return pl.pallas_call(
        attend_kernel,
        out_shape=jax.ShapeDtypeStruct((1344, 512), BF16),
        scratch_shapes=[pltpu.VMEM((64, 64, 512), BF16)]
        + [pltpu.VMEM((4, 2, 64, 512), F32)] * 2 + [pltpu.VMEM((256, 256), F32)] * 2
        + [pltpu.VMEM((256, 256), BF16)] * 2 + [pltpu.VMEM((8, 256), F32)] * 2,
        name="attend",
        compiler_params=pltpu.CompilerParams(vmem_limit_bytes=16 << 20),
        cost_estimate=pl.CostEstimate(flops=5000000000, bytes_accessed=2400000, transcendentals=2800000),
    )(tokens, others, got)


def output_kernel(t_ref, u_ref, a_ref, r_ref, n_ref, own_ref, other_ref, z_ref):
    tokens = jnp.concatenate([t_ref[...], u_ref[...]], axis=1)
    feature = 0.3 * lax.dot_general(r_ref[...], a_ref[...], TN, preferred_element_type=F32)
    feature = feature + 0.7 * lax.dot_general(n_ref[...], tokens, TN, preferred_element_type=F32)
    feature = feature * (1.0 / (0.58 ** 0.5))
    token = lax.broadcasted_iota(jnp.int32, (256, 256), 0)
    lane = lax.broadcasted_iota(jnp.int32, (256, 256), 1)
    keep = lax.rem(token, 16) == lane // 16
    row = lax.broadcasted_iota(jnp.int32, (128, 256), 0)
    lane = lax.broadcasted_iota(jnp.int32, (128, 256), 1)
    for b in range(2):
        part = feature[:, 256 * b:256 * b + 256]
        hi = part.astype(BF16)
        lo = (part - hi.astype(F32)).astype(BF16)
        both = jnp.concatenate([hi, lo], axis=0)
        for i in range(4):
            tile = jnp.where(lax.rem(row, 64) == 16 * i + lax.rem(lane, 16), 1.0, 0.0).astype(BF16)
            wide = lax.dot_general(both, tile, TN, preferred_element_type=F32)
            wide = jnp.where(keep, wide, 0.0).reshape(16, 16, 256)
            wide = jnp.sum(wide, axis=1)
            z_ref[2 * b, pl.ds(i, 16, stride=4), :] = wide[:, :128]
            z_ref[2 * b + 1, pl.ds(i, 16, stride=4), :] = wide[:, 128:]
    own_ref[...] = jnp.concatenate([z_ref[0], z_ref[1]], axis=1)
    other_ref[...] = jnp.concatenate([z_ref[2], z_ref[3]], axis=1).astype(BF16)


def output(tokens, others, attended, r, n):
    return pl.pallas_call(
        output_kernel,
        out_shape=(jax.ShapeDtypeStruct((64, 256), F32), jax.ShapeDtypeStruct((64, 256), BF16)),
        scratch_shapes=[pltpu.VMEM((4, 64, 128), F32)],
        name="output",
        compiler_params=pltpu.CompilerParams(vmem_limit_bytes=12 << 20),
        cost_estimate=pl.CostEstimate(flops=100000000, bytes_accessed=2000000, transcendentals=0),
    )(tokens, others, attended, r, n)


def shards(snap_in, snap_qkv, snap_proj, snap_out, coeffs, latent, levels):
    swap = [(0, 1), (1, 0)]
    keep, give = contract(
        coeffs,
        snap_qkv.transpose(1, 0, 2).reshape(168, 4032),
        snap_proj.transpose(1, 0, 2).reshape(168, 1344),
        snap_in.transpose(2, 0, 1).reshape(168, 64),
        snap_out.transpose(1, 0, 2).reshape(168, 64),
    )
    part = pair_sum(keep, lax.ppermute(give, "core", swap))
    part = a2a(part, ("xh", "xl", "y"))
    send, proj = partial_products(part)
    m, side, n = whole_products(a2a(send, "z"), proj)
    parts = [lax.ppermute(side[d], "y", [(k, (k + d) % 4) for k in range(4)]) for d in range(1, 4)]
    send, latent, levels = lax.optimization_barrier((spread(side, parts, n, m), latent, levels))
    got = a2a(send, ZY)

    c_in, c_skip, c_out = noise_scales(levels)
    tokens = (c_in[:, None, None] * latent).astype(BF16)
    tokens = tokens.reshape(16, 4, 16, 16).transpose(1, 3, 0, 2).reshape(64, 256)
    others = lax.ppermute(tokens, "xl", swap)
    n = got[:, 85].reshape(64, 64)
    r = jnp.concatenate([got[:, 64:85, :64], got[:, 64:85, 64:]], axis=0).reshape(1344, 64)
    attended = attend(tokens, others, got)
    own, other = output(tokens, others, attended, r, n)
    other = lax.ppermute(other, "xl", swap).astype(F32)
    first = lax.axis_index("xl") == 0
    feature = jnp.stack([jnp.where(first, own, other), jnp.where(first, other, own)])
    out = c_skip[:, None, None] * latent + c_out[:, None, None] * feature
    return out[:, None]


def solution(mesh):
    fine = Mesh(mesh.devices.reshape(2, 2, 2, 8, 4), ("xh", "core", "xl", "z", "y"))
    in_specs = (
        P(SNAP, None, PARAM),
        P(SNAP, PARAM, None),
        P(SNAP, PARAM, None),
        P(SNAP, PARAM, None),
        P(SNAP, None),
        P(PARAM, None, None),
        P(PARAM),
    )
    out_specs = P(SNAP, PARAM, None, None)
    return jax.shard_map(shards, mesh=fine, in_specs=in_specs, out_specs=out_specs, check_vma=False)
```

```python
import jax
import jax.numpy as jnp
from jax import lax
from jax.experimental import pallas as pl
from jax.experimental.pallas import tpu as pltpu
from jax.sharding import Mesh, PartitionSpec as P

HEAD_DIM = 64
PROF = 8
NLEV = 16
EPS = 0.0001
LOG2E = 1.4426950408889634

SNAP = ("xh", "core")
PARAM = ("xl", "z", "y")
ZY = ("z", "y")
X = ("xh", "xl")
F32 = jnp.float32
BF16 = jnp.bfloat16
TN = (((0,), (0,)), ((), ()))


def noise_scales(levels):
    step = levels.astype(jnp.float32) / (NLEV - 1)
    sigma = jnp.exp(jnp.log(0.2) + step * (jnp.log(5.0) - jnp.log(0.2)))
    square = sigma * sigma + 0.25
    return (1.0 / jnp.sqrt(square), 0.25 / square, 0.5 * sigma / jnp.sqrt(square))


def a2a(x, axis):
    return lax.all_to_all(x, axis, 0, 0, tiled=True)


def contract_kernel(c_hbm, q_hbm, p_hbm, i_hbm, o_hbm, keep_ref, give_ref, q_ref, p_ref, i_ref,
                    o_ref, h_ref, c_ref, sems):
    pairs = [(c_hbm, c_ref), (i_hbm, i_ref), (o_hbm, o_ref), (p_hbm, p_ref), (q_hbm, q_ref)]
    copies = [pltpu.make_async_copy(a, b, sems.at[k]) for k, (a, b) in enumerate(pairs)]
    for copy in copies:
        copy.start()
    copies[0].wait()
    snap = lax.broadcasted_iota(jnp.int32, (8, 168), 0)
    col = lax.broadcasted_iota(jnp.int32, (8, 168), 1)
    pick = jnp.where(lax.rem(col, 8) == snap, 1.0, 0.0)
    rows = lax.dot_general(c_ref[...], pick, TN, precision=lax.Precision.HIGHEST,
                           preferred_element_type=F32)
    r = lax.broadcasted_iota(jnp.int32, (24, 168), 0)
    col = lax.broadcasted_iota(jnp.int32, (24, 168), 1)
    same = jnp.where(col // 8 == r, 1.0, 0.0)
    mine = lax.axis_index("core")
    picked = []
    for k in range(2):
        for slot in range(4):
            p = (slot // 2) * 4 + slot % 2
            picked.append(jnp.where(mine == k, rows[p:p + 1], rows[p + 2:p + 3]))
    mix = jnp.concatenate([row * same for row in picked], axis=0)
    mix_hi = mix.astype(BF16)
    mix_lo = (mix - mix_hi.astype(F32)).astype(BF16)

    def piece(x):
        hi = x.astype(BF16)
        lo = (x - hi.astype(F32)).astype(BF16)
        y = jnp.dot(mix_hi, hi, preferred_element_type=F32)
        y = y + jnp.dot(mix_hi, lo, preferred_element_type=F32)
        y = y + jnp.dot(mix_lo, hi, preferred_element_type=F32)
        return y.astype(BF16)

    def store(y, blocks, at):
        width = y.shape[1]
        for k, ref in enumerate((keep_ref, give_ref)):
            for slot in range(4):
                row = 96 * k + 24 * slot
                for block in blocks:
                    ref[4 * slot + block, :, at:at + width] = y[row:row + 24]

    copies[1].wait()
    copies[2].wait()
    store(piece(jnp.concatenate([i_ref[...], o_ref[...]], axis=1)), range(4), 1408)
    copies[3].wait()
    for start, width in ((0, 512), (512, 512), (1024, 320)):
        h_ref[:, start:start + width] = piece(p_ref[:, start:start + width])
    source = lax.broadcasted_iota(jnp.int32, (1344, 384), 0)
    col = lax.broadcasted_iota(jnp.int32, (1, 384), 1)
    r = lax.rem(col, 24)
    for block in range(4):
        want = jnp.where(r < 21, (col // 24) * 84 + block * 21 + r, -1)
        order = jnp.where(source == want, 1.0, 0.0).astype(BF16)
        y = jnp.dot(h_ref[...], order, preferred_element_type=F32).astype(BF16)
        store(y, (block,), 1024)
    for k in range(8):
        if k == 0:
            copies[4].wait()
        width = 512 if k < 7 else 448
        store(piece(q_ref[:, 512 * k:512 * k + width]), (k // 2,), 512 * (k % 2))
    for slot in range(4):
        for ref in (keep_ref, give_ref):
            ref[4 * slot + 3, :, 960:1024] = jnp.zeros((24, 64), BF16)


VMEM = pl.BlockSpec(memory_space=pltpu.VMEM)
HBM = pl.BlockSpec(memory_space=pltpu.HBM)


def contract(coeffs, q, p, w_in, w_out):
    shape = jax.ShapeDtypeStruct((16, 24, 1536), BF16)
    return pl.pallas_call(
        contract_kernel,
        out_shape=(shape, shape),
        in_specs=[HBM] * 5,
        out_specs=(VMEM, VMEM),
        scratch_shapes=[pltpu.VMEM((168, 4032), F32), pltpu.VMEM((168, 1344), F32),
                        pltpu.VMEM((168, 64), F32), pltpu.VMEM((168, 64), F32),
                        pltpu.VMEM((192, 1344), BF16), pltpu.VMEM((8, 8), F32),
                        pltpu.SemaphoreType.DMA((5,))],
        name="contract",
        compiler_params=pltpu.CompilerParams(vmem_limit_bytes=16 << 20),
        cost_estimate=pl.CostEstimate(flops=3 * 2 * 192 * 168 * 5504, bytes_accessed=6000000,
                                      transcendentals=0),
    )(*[pltpu.with_memory_space_constraint(x, pltpu.HBM) for x in (coeffs, q, p, w_in, w_out)])


def pair_kernel(a_ref, b_ref, o_ref):
    for k in range(16):
        o_ref[k] = (a_ref[k].astype(F32) + b_ref[k].astype(F32)).astype(BF16)


def pair_sum(a, b):
    return pl.pallas_call(
        pair_kernel,
        out_shape=jax.ShapeDtypeStruct((16, 24, 1536), BF16),
        name="pair",
        compiler_params=pltpu.CompilerParams(vmem_limit_bytes=8 << 20),
        cost_estimate=pl.CostEstimate(flops=600000, bytes_accessed=3600000, transcendentals=0),
    )(a, b)


def lines(values, count, width):
    hi = values.astype(BF16).astype(F32)
    lo = values - hi
    parts = [x[:, width * k:width * k + width] for x in (hi, lo) for k in range(count)]
    row = lax.broadcasted_iota(jnp.int32, (8, width), 0)
    out = jnp.zeros((8, width), F32)
    for k, part in enumerate(parts):
        out = jnp.where(row == k, part, out)
    return out


def unlines(rows, count):
    return jnp.concatenate([rows[k:k + 1] + rows[count + k:count + k + 1] for k in range(count)],
                           axis=1)


def partial_kernel(g_ref, o_ref, p_ref):
    total = (g_ref[0:8].astype(F32) + g_ref[8:16].astype(F32)).reshape(192, 1536)
    w_in = total[:, 1408:1472]
    norm = jnp.sqrt(jnp.sum(w_in * w_in, axis=1, keepdims=True))
    w_in = (w_in / (EPS + norm)).astype(BF16)
    w_out = total[:, 1472:1536].astype(BF16)
    n = lax.dot_general(w_in, w_out, TN, preferred_element_type=F32)
    proj = total[:, 1024:1408]
    p_ref[...] = proj
    y = lax.axis_index("y")
    own = [g_ref[4 * x + y].astype(F32) + g_ref[8 + 4 * x + y].astype(F32) for x in range(2)]
    own = jnp.concatenate([x[:, 1472:1536] for x in own], axis=1)
    low = jnp.concatenate([own, lines(jnp.sum(proj * proj, axis=0, keepdims=True), 3, 128)], axis=0)
    for z in range(8):
        q = total[:, 128 * z:128 * z + 128]
        m = lax.dot_general(w_in, q.astype(BF16), TN, preferred_element_type=F32)
        side = lines(jnp.sum(q * q, axis=0, keepdims=True), 2, 64)
        tail = jnp.concatenate([n[8 * z:8 * z + 8], side], axis=1)
        o_ref[z] = jnp.concatenate([m, tail, low], axis=0).astype(BF16)


def partial_products(got):
    return pl.pallas_call(
        partial_kernel,
        out_shape=(jax.ShapeDtypeStruct((8, 104, 128), BF16),
                   jax.ShapeDtypeStruct((192, 384), F32)),
        name="partial",
        compiler_params=pltpu.CompilerParams(vmem_limit_bytes=8 << 20),
        cost_estimate=pl.CostEstimate(flops=2 * 64 * 192 * 1152, bytes_accessed=1000000,
                                      transcendentals=0),
    )(got)


def rows_kernel(g_ref, p_ref, r_ref, n_ref):
    total = g_ref[0, 64:104].astype(F32)
    for z in range(1, 8):
        total = total + g_ref[z, 64:104].astype(F32)
    n_ref[...] = total[0:8]
    w_out = g_ref[:, 72:96, :].astype(F32).reshape(192, 128)
    w_out = jnp.concatenate([w_out[:, :64], w_out[:, 64:]], axis=0)
    norm = jnp.sqrt(unlines(total[32:40], 3))
    proj = (p_ref[...] / (EPS + norm)).astype(BF16)
    r = jnp.dot(proj, w_out.astype(BF16), preferred_element_type=F32)
    square = lines(jnp.sum(w_out * w_out, axis=0, keepdims=True), 1, 64)
    square = jnp.concatenate([square, square], axis=1)
    mine = lax.axis_index("y")
    for y in range(4):
        both = jnp.concatenate([r[24 * y:24 * y + 24], r[96 + 24 * y:120 + 24 * y]], axis=1)
        r_ref[lax.rem(y + 4 - mine, 4)] = jnp.concatenate([both, square], axis=0).astype(BF16)


def row_products(got, proj):
    return pl.pallas_call(
        rows_kernel,
        out_shape=(jax.ShapeDtypeStruct((4, 32, 128), BF16),
                   jax.ShapeDtypeStruct((8, 128), F32)),
        name="rows",
        compiler_params=pltpu.CompilerParams(vmem_limit_bytes=8 << 20),
        cost_estimate=pl.CostEstimate(flops=100000, bytes_accessed=800000, transcendentals=0),
    )(got, proj)


def units_kernel(g_ref, o_ref):
    total = g_ref[0, 0:72].astype(F32)
    for z in range(1, 8):
        total = total + g_ref[z, 0:72].astype(F32)
    o_ref[...] = total[0:64] / (EPS + jnp.sqrt(unlines(total[64:72, 64:128], 2)))


def unit_products(got):
    return pl.pallas_call(
        units_kernel,
        out_shape=jax.ShapeDtypeStruct((64, 128), F32),
        name="units",
        compiler_params=pltpu.CompilerParams(vmem_limit_bytes=4 << 20),
        cost_estimate=pl.CostEstimate(flops=100000, bytes_accessed=200000, transcendentals=0),
    )(got)


def spread_kernel(a_ref, b_ref, c_ref, d_ref, n_ref, m_ref, o_ref):
    total = a_ref[0].astype(F32)
    for ref in (b_ref, c_ref, d_ref):
        total = total + ref[...].astype(F32)
    scale = 1.0 / (EPS + jnp.sqrt(total[24:25] + total[25:26]))
    n = n_ref[...]
    mine = lax.axis_index("y")
    line = jnp.zeros((1, 128), F32)
    for y in range(4):
        pair = jnp.concatenate([n[2 * y:2 * y + 1, :64], n[2 * y + 1:2 * y + 2, :64]], axis=1)
        line = jnp.where(mine == y, pair, line)
    row = lax.broadcasted_iota(jnp.int32, (24, 128), 0)
    r = jnp.where(row == 21, line, total[:24]) * scale
    out = jnp.concatenate([m_ref[...], r], axis=0).astype(BF16)
    for k in range(32):
        o_ref[k] = out


def spread(side, parts, n, m):
    return pl.pallas_call(
        spread_kernel,
        out_shape=jax.ShapeDtypeStruct((32, 88, 128), BF16),
        name="spread",
        compiler_params=pltpu.CompilerParams(vmem_limit_bytes=4 << 20),
        cost_estimate=pl.CostEstimate(flops=20000, bytes_accessed=800000, transcendentals=0),
    )(side, *parts, n, m)


def attend_kernel(t_ref, b_ref, r_ref, n_ref, o_ref, a_ref, z_ref, s_ref, x0_ref, x1_ref, c0_ref,
                  c1_ref, e0_ref, e1_ref, d0_ref, d1_ref):
    tokens = t_ref[...]
    blocks, scores, expos, sums = (x0_ref, x1_ref), (c0_ref, c1_ref), (e0_ref, e1_ref), (d0_ref, d1_ref)

    def columns(g):
        for k in range(4):
            x = lax.dot_general(b_ref[4 * g + k, 0:64, :], tokens, TN, preferred_element_type=F32)
            blocks[g % 2][k] = x.reshape(2, 64, 256)

    def unit(g):
        squares = []
        for k in range(4):
            x = blocks[g % 2][k]
            squares.append(jnp.sum(x * x, axis=1))
        scale = jnp.sqrt(jnp.concatenate(squares, axis=0) * (1.0 / 64))
        scale = 1.0 / (EPS + scale)
        for k in range(4):
            for half in range(2):
                row = scale[2 * k + half:2 * k + half + 1]
                s_ref[16 * k + 2 * g + half] = (blocks[g % 2][k, half] * row).astype(BF16)

    columns(0)
    columns(1)
    for g in range(8):
        unit(g)
        if g + 2 < 8:
            columns(g + 2)

    def score(h):
        scores[h % 2][...] = lax.dot_general(s_ref[21 + h], s_ref[h], TN, preferred_element_type=F32)

    def weigh(h):
        expo = jnp.exp2(scores[h % 2][...] * (0.125 * LOG2E))
        expos[h % 2][...] = expo.astype(BF16)
        sums[h % 2][...] = jnp.sum(expo.reshape(32, 8, 256), axis=0)

    def gather(h):
        out = jnp.dot(s_ref[42 + h], expos[h % 2][...], preferred_element_type=F32)
        total = jnp.sum(sums[h % 2][...], axis=0, keepdims=True)
        a_ref[64 * h:64 * h + 64, :] = (out * (1.0 / total)).astype(BF16)

    score(0)
    score(1)
    for h in range(21):
        weigh(h)
        if h > 0:
            gather(h - 1)
        if h + 2 < 21:
            score(h + 2)
    gather(20)

    feature = 0.3 * lax.dot_general(r_ref[...], a_ref[...], TN, preferred_element_type=F32)
    feature = feature + 0.7 * lax.dot_general(n_ref[...], tokens, TN, preferred_element_type=F32)
    feature = feature * (1.0 / (0.58 ** 0.5))
    token = lax.broadcasted_iota(jnp.int32, (256, 256), 0)
    lane = lax.broadcasted_iota(jnp.int32, (256, 256), 1)
    keep = lax.rem(token, 16) == lane // 16
    row = lax.broadcasted_iota(jnp.int32, (128, 256), 0)
    lane = lax.broadcasted_iota(jnp.int32, (128, 256), 1)
    hi = feature.astype(BF16)
    lo = (feature - hi.astype(F32)).astype(BF16)
    both = jnp.concatenate([hi, lo], axis=0)
    for i in range(4):
        tile = jnp.where(lax.rem(row, 64) == 16 * i + lax.rem(lane, 16), 1.0, 0.0).astype(BF16)
        wide = lax.dot_general(both, tile, TN, preferred_element_type=F32)
        wide = jnp.where(keep, wide, 0.0).reshape(16, 16, 256)
        wide = jnp.sum(wide, axis=1)
        z_ref[0, pl.ds(i, 16, stride=4), :] = wide[:, :128]
        z_ref[1, pl.ds(i, 16, stride=4), :] = wide[:, 128:]
    o_ref[...] = jnp.concatenate([z_ref[0], z_ref[1]], axis=1).astype(o_ref.dtype)


def attend(tokens, got, r, n, dtype):
    return pl.pallas_call(
        attend_kernel,
        out_shape=jax.ShapeDtypeStruct((64, 256), dtype),
        scratch_shapes=[pltpu.VMEM((1344, 256), BF16), pltpu.VMEM((2, 64, 128), F32),
                        pltpu.VMEM((64, 64, 256), BF16)]
        + [pltpu.VMEM((4, 2, 64, 256), F32)] * 2 + [pltpu.VMEM((256, 256), F32)] * 2
        + [pltpu.VMEM((256, 256), BF16)] * 2 + [pltpu.VMEM((8, 256), F32)] * 2,
        name="attend",
        compiler_params=pltpu.CompilerParams(vmem_limit_bytes=12 << 20),
        cost_estimate=pl.CostEstimate(flops=2500000000, bytes_accessed=1200000, transcendentals=1400000),
    )(tokens, got, r, n)


def shards(snap_in, snap_qkv, snap_proj, snap_out, coeffs, latent, levels):
    swap = [(0, 1), (1, 0)]
    keep, give = contract(
        coeffs,
        snap_qkv.transpose(1, 0, 2).reshape(168, 4032),
        snap_proj.transpose(1, 0, 2).reshape(168, 1344),
        snap_in.transpose(2, 0, 1).reshape(168, 64),
        snap_out.transpose(1, 0, 2).reshape(168, 64),
    )
    part = pair_sum(keep, lax.ppermute(give, "core", swap))
    part = a2a(part, ("xh", "xl", "y"))
    send, proj = partial_products(part)
    got = a2a(send, "z")
    side, n = row_products(got, proj)
    parts = [lax.ppermute(side[d], "y", [(k, (k + d) % 4) for k in range(4)]) for d in range(1, 4)]
    send = spread(side, parts, n, unit_products(got))
    send, latent, levels = lax.optimization_barrier((send, latent, levels))
    got = a2a(send, ZY)

    c_in, c_skip, c_out = noise_scales(levels)
    tokens = (c_in[:, None, None] * latent).astype(BF16)
    tokens = tokens.reshape(16, 4, 16, 16).transpose(1, 3, 0, 2).reshape(64, 256)
    others = lax.ppermute(tokens, "xl", swap)
    n = got[:, 85].reshape(64, 64)
    r = jnp.concatenate([got[:, 64:85, :64], got[:, 64:85, 64:]], axis=0).reshape(1344, 64)
    other = attend(others, got, r, n, BF16)
    tokens, other = lax.optimization_barrier((tokens, other))
    other = lax.ppermute(other, "xl", swap).astype(F32)
    own = attend(tokens, got, r, n, F32)
    first = lax.axis_index("xl") == 0
    feature = jnp.stack([jnp.where(first, own, other), jnp.where(first, other, own)])
    out = c_skip[:, None, None] * latent + c_out[:, None, None] * feature
    return out[:, None]


def solution(mesh):
    fine = Mesh(mesh.devices.reshape(2, 2, 2, 8, 4), ("xh", "core", "xl", "z", "y"))
    in_specs = (
        P(SNAP, None, PARAM),
        P(SNAP, PARAM, None),
        P(SNAP, PARAM, None),
        P(SNAP, PARAM, None),
        P(SNAP, None),
        P(PARAM, None, None),
        P(PARAM),
    )
    out_specs = P(SNAP, PARAM, None, None)
    return jax.shard_map(shards, mesh=fine, in_specs=in_specs, out_specs=out_specs, check_vma=False)
```
